256 devices in a mesh: dp: 16 (over x_lo, y, core), index: 16 (over z, x_hi).
Axes of the slice: x: 4 (x_hi: 2, x_lo: 2; x = x_hi * 2 + x_lo), y: 4, z: 8, core: 2. Of those that a mesh axis runs over, the one named last changes fastest.
Arguments:
- queries: bfloat16 [32768, 1024], P(('dp', 'index')), may hold values from -0.1875 to 0.1875
- keys: bfloat16 [16384, 1024], P(('dp', 'index')), may hold values from -6 to 6
- pattern: int32 [256, 256], P(('dp', 'index')), may hold values 0 or 1
- clusters: int32 [16384], P(('dp', 'index')), may hold values from 0 to 255
- positives: int32 [32768], P(('dp', 'index')), may hold values from 0 to 16383
- loss_multiplier: float32 [32768], P(('dp', 'index')), may hold values from -4 to 4
Outputs:
- query_grad: float32 [32768, 1024], P(('dp', 'index'))
- loss: float32 [32768], P(('dp', 'index'))
The draws below stay inside these ranges and needn't reach their ends.
All inputs are finite; a program needn't handle non-finite values. No bound on the sum of `pattern` on one device may be relied on, other than what follows from the above.
Results may differ from the reference program's by a relative error of at most 0.0029.
Values may be sent and summed in bfloat16 or wider, within the bound.
A program may use at most 64 MiB of HBM per device.

```python
import math
import jax
import jax.numpy as jnp
from jax import lax

D = 1024
QBLK = 128
NCB = 256
NQ = 32768
NQB = 256
NKEYS = 16384


def with_ends(array, key, least, high):
    longest = array.shape.index(max(array.shape))
    spots = []
    for shift in (0, 1):
        where = [jax.random.randint(jax.random.fold_in(key, axis), (), 0, length) for axis, length in enumerate(array.shape)]
        where[longest] = (where[longest] + shift) % array.shape[longest]
        spots.append(tuple(where))
    return array.at[spots[0]].set(least).at[spots[1]].set(high)


def block_levels(stream_key, extent, cuts, smallest, top_value):
    factor_of = 1.0
    for axis_at, shards_of in cuts:
        heights = jax.random.uniform(jax.random.fold_in(jax.random.fold_in(stream_key, 6), axis_at), (shards_of,), jnp.float32, smallest / len(cuts), top_value / len(cuts))
        factor_of = factor_of * jnp.repeat(jnp.exp(heights), extent[axis_at] // shards_of).reshape((-1,) + (1,) * (len(extent) - 1 - axis_at))
    return factor_of


def normal_values(stream_key, extent, width, reach, cuts=(), kind=jnp.bfloat16):
    gain = block_levels(stream_key, extent, cuts, -0.22, 0.18) if cuts else 1.0
    result = jax.random.normal(stream_key, extent, jnp.float32) * width * gain
    return jnp.minimum(jnp.maximum(result, -reach), reach).astype(kind)


def setup_inputs(seed: int = 0) -> dict:
    arg_keys = jax.random.split(jax.random.key(seed), 7)
    queries = normal_values(arg_keys[0], (NQ, D), 0.03125, 0.1875, ((0, 256),))
    keys = normal_values(arg_keys[1], (NKEYS, D), 1.0, 6.0, ((0, 256),))
    pattern = with_ends((jax.random.randint(arg_keys[2], (NQB, NCB), 0, 2) < 1).astype(jnp.int32), jax.random.fold_in(arg_keys[2], 1), 0, 1)
    clusters = with_ends(jax.random.randint(arg_keys[3], (NKEYS,), 0, NCB), jax.random.fold_in(arg_keys[3], 1), 0, NCB - 1).astype(jnp.int32)
    positives = with_ends(jax.random.randint(arg_keys[4], (NQ,), 0, NKEYS), jax.random.fold_in(arg_keys[4], 1), 0, NKEYS - 1).astype(jnp.int32)
    loss_multiplier = normal_values(arg_keys[5], (NQ,), 1.0, 4.0, ((0, 256),), jnp.float32)
    return dict(queries=queries, keys=keys, pattern=pattern, clusters=clusters, positives=positives, loss_multiplier=loss_multiplier)


logit_divisor = 0.1
epsilon = 1e-06

def reference(queries, keys, pattern, clusters, positives, loss_multiplier):
    query_floats = queries.astype(jnp.float32)
    query_scale = lax.rsqrt(lax.optimization_barrier(jnp.sum(query_floats * query_floats, axis=1, keepdims=True)) + epsilon)
    query_norm = (query_floats * query_scale).astype(jnp.bfloat16)
    key_floats = keys.astype(jnp.float32)
    passage_magnitude = (key_floats * lax.rsqrt(lax.optimization_barrier(jnp.sum(key_floats * key_floats, axis=1, keepdims=True)) + epsilon)).astype(jnp.bfloat16)
    key_ids = jnp.arange(NKEYS, dtype=jnp.int32)
    cluster_table = (clusters[:, None] == jnp.arange(NCB, dtype=jnp.int32)[None, :]).astype(jnp.float32)
    block_rows = math.gcd(NQ, 1024)
    block_count = NQ // block_rows

    def one_block(block_index):
        first_row = (block_index * block_rows).astype(jnp.int32)
        question_batch_slab = lax.dynamic_slice_in_dim(query_norm, first_row, block_rows, 0)
        block_marks = lax.dynamic_slice_in_dim(pattern, (first_row // QBLK).astype(jnp.int32), block_rows // QBLK, 0).astype(jnp.float32)
        allowed = jnp.dot(block_marks, cluster_table.T, precision=lax.Precision.HIGHEST)
        allowed = jnp.repeat(allowed, QBLK, axis=0)
        wanted = lax.dynamic_slice_in_dim(positives, first_row, block_rows, 0)
        is_positive = (key_ids[None, :] == wanted[:, None]).astype(jnp.float32)
        inner_product_matrix = jnp.dot(question_batch_slab, passage_magnitude.T, preferred_element_type=jnp.float32) / logit_divisor
        weights = jnp.exp(inner_product_matrix) * jnp.maximum(allowed, is_positive)
        totals = lax.optimization_barrier(jnp.sum(weights, axis=1))
        positive_scores = lax.optimization_barrier(jnp.sum(inner_product_matrix * is_positive, axis=1))
        expected = jnp.dot(weights.astype(jnp.bfloat16), passage_magnitude, preferred_element_type=jnp.float32)
        positive_keys = passage_magnitude[wanted].astype(jnp.float32)
        update_direction_entry = expected / totals[:, None] - positive_keys
        return (update_direction_entry, jnp.log(totals) - positive_scores)
    directions, losses = lax.map(one_block, jnp.arange(block_count, dtype=jnp.int32))
    update_direction_entry = directions.reshape(NQ, D)
    loss_values = losses.reshape(NQ)
    question_derivative = update_direction_entry * (loss_multiplier / logit_divisor)[:, None]
    projection = lax.optimization_barrier(jnp.sum(query_floats * question_derivative, axis=1, keepdims=True))
    query_grad = query_scale * question_derivative - query_scale * query_scale * query_scale * query_floats * projection
    return (query_grad, loss_values)
```

```python
import functools
import math

import jax
import jax.numpy as jnp
from jax import lax
from jax.experimental import pallas as pl
from jax.experimental.pallas import tpu as pltpu
from jax.sharding import PartitionSpec as P

MESH = pl.DeviceIdType.MESH
EPS = 1e-06
NX, NY, NZ = 4, 4, 8
EXP2_SCALE = 10.0 * math.log2(math.e)
F32, BF16, I32 = jnp.float32, jnp.bfloat16, jnp.int32


def unit_of(k):
    if k == 0:
        return 0
    if k == 4:
        return 14
    return 2 + 4 * (k - 1) if k < 4 else 2 + 4 * (7 - k) + 1


def sibling_unit(k):
    return unit_of(k) + (1 if k in (0, 4) else 2)


class Ids:
    def __init__(self):
        self.names = {}

    def __call__(self, *name):
        return self.names.setdefault(name, len(self.names))


def message_names():
    ids = Ids()
    for d in (1, 2, 3):
        ids("x0", d), ids("cx", d), ids("meta", d), ids("tot", d), ids("out", d)
    for name in (("q", 1), ("q", 3), ("q2", 1), ("q2", 3), ("cs",)):
        ids(*name)
    for k in range(1, 8):
        ids("cz", k), ids("bz", k)
        for d in (1, 2, 3):
            ids("bx", k, d)
        if k != 4:
            ids("az", k)
    ids("az", 4, 0), ids("az", 4, 1)
    for k in range(8):
        ids("sib", k)
    return ids


IDS = message_names()


def kernel(q_ref, k_ref, meta_ref, cl_ref, lm_ref, og_ref, ol_ref, kb, qb, mb, clx, clz, pm, amb,
           wbuf, obuf, sbuf, e_acc, p_acc, pos_t, tot, pss, tb, pb, rb, ssem, rsem):
    dp, ix = lax.axis_index("dp"), lax.axis_index("index")
    c, y, x, z = dp % 2, (dp // 2) % NY, (ix % 2) * 2 + dp // (2 * NY), ix // 2

    def dev(xx, yy, zz, cc):
        return ((xx % 2) * NY + yy) * 2 + cc, zz * 2 + xx // 2

    def at_x(d):
        return dev((x + d + NX) % NX, y, z, c)

    def at_y(d):
        return dev(x, (y + d + NY) % NY, z, c)

    def at_z(d):
        return dev(x, y, (z + d + NZ) % NZ, c)

    sibling = dev(x, y, z, 1 - c)
    partners = [at_x(d) for d in (1, 2, 3)] + [at_y(d) for d in (1, 2, 3)] + [at_z(d) for d in range(1, 8)] + [sibling]

    barrier = pltpu.get_barrier_semaphore()
    for partner in partners:
        pl.semaphore_signal(barrier, inc=1, device_id=partner, device_id_type=MESH)

    copies = {}

    def send(name, src, dst, target):
        number = IDS.names[name]
        copy = pltpu.make_async_remote_copy(
            src_ref=src, dst_ref=dst, send_sem=ssem.at[number], recv_sem=rsem.at[number],
            device_id=target, device_id_type=MESH)
        copy.start()
        copies[name] = copy

    def arrived(*name):
        copies[name].wait_recv()

    kf = k_ref[...].astype(F32)
    kn = (kf * lax.rsqrt(jnp.sum(kf * kf, axis=1, keepdims=True) + EPS)).astype(BF16)
    kb[0, 0] = kn[:32]
    kb[0, 1] = kn[32:]
    xf = q_ref[...].astype(F32)
    qb[0] = (xf * lax.rsqrt(jnp.sum(xf * xf, axis=1, keepdims=True) + EPS)).astype(BF16)
    mb[0] = meta_ref[...]
    clx[0] = cl_ref[...]

    pl.semaphore_wait(barrier, len(partners))

    for d in (1, 3, 2):
        send(("x0", d), kb.at[0], kb.at[d], at_x(d))
    send(("bz", 1), kb.at[0, 1], kb.at[unit_of(1) * 4, 1], at_z(1))
    send(("bz", 7), kb.at[0, 1], kb.at[unit_of(7) * 4, 1], at_z(-1))
    send(("q", 1), qb.at[0], qb.at[1], at_y(1))
    send(("q", 3), qb.at[0], qb.at[3], at_y(-1))
    for d in (1, 2, 3):
        send(("meta", d), mb.at[0], mb.at[d], at_y(d))
        send(("cx", d), clx.at[0], clx.at[d], at_x(d))

    for d in (1, 2, 3):
        arrived("cx", d)
    lane = lax.broadcasted_iota(I32, (1, 256), 1)
    row = clx[0]
    for d in (1, 2, 3):
        row = jnp.where(lane // 64 == d, clx[d], row)
    clz[0, 0] = row
    for k in range(1, 8):
        send(("cz", k), clz.at[0, 0], clz.at[0, k], at_z(k))

    for d in (1, 2, 3):
        arrived("x0", d)
    send(("az", 1), kb.at[0:4, 0], kb.at[pl.ds(unit_of(1) * 4, 4), 0], at_z(1))
    send(("az", 7), kb.at[0:4, 0], kb.at[pl.ds(unit_of(7) * 4, 4), 0], at_z(-1))
    send(("sib", 0), kb.at[0:4], kb.at[pl.ds(sibling_unit(0) * 4, 4)], sibling)

    def a_half(k):
        return kb.at[pl.ds(unit_of(k) * 4, 4), 0]

    def b_half(k, j):
        return kb.at[unit_of(k) * 4 + j, 1]

    def forward(r):
        ks = (r, 8 - r) if r < 4 else (4,)
        for k in ks:
            arrived("bz", k)
            if k < 4:
                send(("bz", k + 1), b_half(k, 0), b_half(k + 1, 0), at_z(1))
            elif k > 5:
                send(("bz", k - 1), b_half(k, 0), b_half(k - 1, 0), at_z(-1))
            send(("bx", k, 1), b_half(k, 0), b_half(k, 1), at_x(1))
            send(("bx", k, 3), b_half(k, 0), b_half(k, 3), at_x(-1))
        if r < 4:
            arrived("az", r)
            if r < 3:
                send(("az", r + 1), a_half(r), a_half(r + 1), at_z(1))
            else:
                send(("az", 4, 0), kb.at[pl.ds(unit_of(3) * 4, 2), 0], kb.at[pl.ds(unit_of(4) * 4, 2), 0], at_z(1))
            arrived("az", 8 - r)
            if r < 3:
                send(("az", 7 - r), a_half(8 - r), a_half(7 - r), at_z(-1))
            else:
                send(("az", 4, 1), kb.at[pl.ds(unit_of(5) * 4 + 2, 2), 0],
                     kb.at[pl.ds(unit_of(4) * 4 + 2, 2), 0], at_z(-1))
        else:
            arrived("az", 4, 0)
            arrived("az", 4, 1)
        for k in ks:
            arrived("bx", k, 1)
            arrived("bx", k, 3)
            if k % 2 == 0:
                send(("bx", k, 2), b_half(k, 1), b_half(k, 2), at_x(1))
            else:
                send(("bx", k, 2), b_half(k, 3), b_half(k, 2), at_x(-1))

    def share(r):
        for k in (r, 8 - r) if r < 4 else (4,):
            arrived("bx", k, 2)
            send(("sib", k), kb.at[pl.ds(unit_of(k) * 4, 4)], kb.at[pl.ds(sibling_unit(k) * 4, 4)], sibling)

    def queries_on():
        arrived("q", 1)
        send(("q2", 1), qb.at[1, 0:64], qb.at[2, 0:64], at_y(1))
        arrived("q", 3)
        send(("q2", 3), qb.at[3, 64:128], qb.at[2, 64:128], at_y(-1))

    def prepare():
        for k in range(1, 8):
            arrived("cz", k)
        send(("cs",), clz.at[0], clz.at[1], sibling)
        pm[...] = jnp.zeros_like(pm)
        for d in range(4):
            if d:
                arrived("meta", d)
            pm[d:d + 1, :] = mb[d, :, 0:256].astype(F32)
            pos = jnp.broadcast_to(mb[d, :, 256:384].astype(F32), (128, 128))
            pos_t[d * 128:(d + 1) * 128, :] = pos.T
        tot[...] = jnp.zeros_like(tot)
        pss[...] = jnp.zeros_like(pss)
        arrived("cs")
        arrived("q2", 1)
        arrived("q2", 3)

    def compute(r):
        ks = (r, 8 - r) if 0 < r < 4 else (r,)
        for k in ks:
            arrived("sib", k)
        units = 2 * len(ks)
        first = unit_of(r)

        def unit_step(t, carry):
            if units == 2:
                s, k = t, r
            else:
                s, k = t // 2, r + (t % 2) * (8 - 2 * r)
            keys = kb[pl.ds((first + t) * 4, 4)].reshape(256, 1024)
            sbuf[...] = lax.dot_general(qb[...].reshape(512, 1024), keys, (((1,), (1,)), ((), ())),
                                        preferred_element_type=F32)
            lanes = lax.broadcasted_iota(I32, (1, 256), 1)
            xx = (x - lanes // 64 + NX) % NX
            zz = (z - k + NZ) % NZ
            cc = c + s - 2 * c * s
            rank = (((xx % 2) * NY + y) * 2 + cc) * 16 + zz * 2 + xx // 2
            key_id = (rank * 64 + lanes % 64).astype(F32)
            hot = (lax.broadcasted_iota(I32, (256, 256), 0) == clz[s, k]).astype(F32).astype(BF16)
            amb[...] = lax.dot_general(pm[...].astype(BF16), hot, (((1,), (0,)), ((), ())),
                                       preferred_element_type=F32)
            for b in range(4):
                rows = slice(b * 128, (b + 1) * 128)
                for h in range(2):
                    cols = slice(h * 128, (h + 1) * 128)
                    st = sbuf[rows, cols]
                    is_pos = pos_t[rows, :] == key_id[:, cols]
                    one = jnp.where(is_pos, 1.0, 0.0)
                    w = jnp.exp2(st * EXP2_SCALE) * jnp.maximum(one, amb[b:b + 1, cols])
                    tot[rows, :] += w
                    pss[rows, :] += st * one
                    to = pl.ds(pl.multiple_of(t * 256 + h * 128, 128), 128)
                    wbuf[rows, to] = w.astype(BF16)
                    obuf[rows, to] = one.astype(BF16)
            return carry

        lax.fori_loop(0, units, unit_step, 0)

        def column_step(n, carry):
            cols = pl.ds(pl.multiple_of(n * 256, 256), 256)
            keys = kb[first * 4:(first + units) * 4, :, :, cols].reshape(units * 256, 256)
            e_new = jnp.dot(wbuf[:, 0:units * 256], keys, preferred_element_type=F32)
            p_new = jnp.dot(obuf[:, 0:units * 256], keys, preferred_element_type=F32)
            if r == 0:
                e_acc[:, cols] = e_new
                p_acc[:, cols] = p_new
            else:
                e_acc[:, cols] += e_new
                p_acc[:, cols] += p_new
            return carry

        lax.fori_loop(0, 4, column_step, 0)

    forward(1)
    queries_on()
    forward(2)
    share(1)
    prepare()
    compute(0)
    forward(3)
    share(2)
    compute(1)
    forward(4)
    share(3)
    compute(2)
    share(4)
    compute(3)
    compute(4)

    for b in range(4):
        rows = slice(b * 128, (b + 1) * 128)
        tb[0, b:b + 1, :] = jnp.sum(tot[rows, :].T, axis=0, keepdims=True)
        tb[0, 4 + b:5 + b, :] = jnp.sum(pss[rows, :].T, axis=0, keepdims=True)
    for d in (2, 1, 3):
        send(("tot", d), tb.at[0], tb.at[d], at_y(d))
    for d in (1, 3, 2):
        arrived("tot", d)

    def total_row(b, base):
        row = tb[0, base + b:base + b + 1, :]
        for d in (1, 2, 3):
            i = base + (b - d) % 4
            row = row + tb[d, i:i + 1, :]
        return row

    def partial_rows(b):
        inverse = (1.0 / jnp.broadcast_to(total_row(b, 0), (128, 128)).T)[:, 0:1]
        rows = slice(b * 128, (b + 1) * 128)
        return e_acc[rows, :] * inverse - p_acc[rows, :]

    for b in (2, 1, 3):
        pb[b - 1] = partial_rows(b).astype(BF16)
        send(("out", b), pb.at[b - 1], rb.at[b - 1], at_y(-b))
    ol_ref[...] = jnp.log(total_row(0, 0)) - total_row(0, 4) * 10.0
    og_ref[...] = partial_rows(0)
    for b in (1, 3, 2):
        arrived("out", b)
    direction = og_ref[...] + ((rb[0].astype(F32) + rb[1].astype(F32)) + rb[2].astype(F32))
    scale = (jnp.broadcast_to(lm_ref[...], (128, 128)).T)[:, 0:1] * 10.0
    xf = q_ref[...].astype(F32)
    q_scale = lax.rsqrt(jnp.sum(xf * xf, axis=1, keepdims=True) + EPS)
    g = direction * scale
    projection = jnp.sum(xf * g, axis=1, keepdims=True)
    og_ref[...] = q_scale * g - (q_scale * q_scale * q_scale * projection) * xf
    for copy in copies.values():
        copy.wait_send()


def body(queries, keys, pattern, clusters, positives, loss_multiplier):
    meta = jnp.concatenate([pattern.reshape(1, 256), positives.reshape(1, 128)], axis=1)
    ids = jnp.tile(clusters.reshape(1, 64), (1, 4))
    vmem = pl.BlockSpec(memory_space=pltpu.VMEM)
    count = len(IDS.names)
    grad, loss = pl.pallas_call(
        kernel,
        out_shape=(jax.ShapeDtypeStruct((128, 1024), F32), jax.ShapeDtypeStruct((1, 128), F32)),
        in_specs=[vmem] * 5,
        out_specs=(vmem, vmem),
        scratch_shapes=[
            pltpu.VMEM((64, 2, 32, 1024), BF16),
            pltpu.VMEM((4, 128, 1024), BF16),
            pltpu.VMEM((4, 1, 384), I32),
            pltpu.VMEM((4, 1, 256), I32),
            pltpu.VMEM((2, 8, 1, 256), I32),
            pltpu.VMEM((8, 256), F32),
            pltpu.VMEM((8, 256), F32),
            pltpu.VMEM((512, 1024), BF16),
            pltpu.VMEM((512, 1024), BF16),
            pltpu.VMEM((512, 256), F32),
            pltpu.VMEM((512, 1024), F32),
            pltpu.VMEM((512, 1024), F32),
            pltpu.VMEM((512, 128), F32),
            pltpu.VMEM((512, 128), F32),
            pltpu.VMEM((512, 128), F32),
            pltpu.VMEM((4, 8, 128), F32),
            pltpu.VMEM((3, 128, 1024), BF16),
            pltpu.VMEM((3, 128, 1024), BF16),
            pltpu.SemaphoreType.DMA((count,)),
            pltpu.SemaphoreType.DMA((count,)),
        ],
        compiler_params=pltpu.CompilerParams(
            collective_id=0, has_side_effects=True, vmem_limit_bytes=50 * 1024 * 1024),
        name="contrastive",
    )(queries, keys, meta, ids, loss_multiplier.reshape(1, 128))
    return grad, loss.reshape(128)


def solution(mesh):
    rows, flat = P(("dp", "index"), None), P(("dp", "index"))
    return jax.shard_map(
        body, mesh=mesh, in_specs=(rows, rows, rows, flat, flat, flat), out_specs=(rows, flat), check_vma=False)
```

```python
import functools
import math

import jax
import jax.numpy as jnp
from jax import lax
from jax.experimental import pallas as pl
from jax.experimental.pallas import tpu as pltpu
from jax.sharding import PartitionSpec as P

MESH = pl.DeviceIdType.MESH
EPS = 1e-06
NX, NY, NZ = 4, 4, 8
EXP2_SCALE = 10.0 * math.log2(math.e)
F32, BF16, I32 = jnp.float32, jnp.bfloat16, jnp.int32


def unit_of(k):
    if k == 0:
        return 0
    if k == 4:
        return 14
    return 2 + 4 * (k - 1) if k < 4 else 2 + 4 * (7 - k) + 1


def sibling_unit(k):
    return unit_of(k) + (1 if k in (0, 4) else 2)


class Ids:
    def __init__(self):
        self.names = {}

    def __call__(self, *name):
        return self.names.setdefault(name, len(self.names))


def message_names():
    ids = Ids()
    for d in (1, 2, 3):
        ids("xa", d), ids("xb", d), ids("cx", d), ids("meta", d), ids("tot", d), ids("out", d)
    for name in (("q", 1), ("q", 3), ("q2", 1), ("q2", 3), ("cs",)):
        ids(*name)
    for k in range(1, 8):
        ids("cz", k), ids("f", k)
        for d in (1, 2, 3):
            ids("bx", k, d), ids("g", k, d)
    for k in range(8):
        ids("sib", k)
    return ids


IDS = message_names()


def kernel(q_ref, k_ref, pat_ref, cl_ref, pos_ref, lm_ref, og_ref, ol_ref, kin, qin, clv, lmv, kb, qb, mb, clx, clz,
           pm, amb, wbuf, obuf, sbuf, e_acc, p_acc, pos_t, tot, pss, tb, pb, rb, lsem, ssem, rsem):
    dp, ix = lax.axis_index("dp"), lax.axis_index("index")
    c, y, x, z = dp % 2, (dp // 2) % NY, (ix % 2) * 2 + dp // (2 * NY), ix // 2

    def dev(xx, yy, zz, cc):
        return ((xx % 2) * NY + yy) * 2 + cc, zz * 2 + xx // 2

    def at_x(d):
        return dev((x + d + NX) % NX, y, z, c)

    def at_y(d):
        return dev(x, (y + d + NY) % NY, z, c)

    def at_z(d):
        return dev(x, y, (z + d + NZ) % NZ, c)

    sibling = dev(x, y, z, 1 - c)
    partners = [at_x(d) for d in (1, 2, 3)] + [at_y(d) for d in (1, 2, 3)] + [at_z(d) for d in range(1, 8)] + [sibling]

    barrier = pltpu.get_barrier_semaphore()
    for partner in partners:
        pl.semaphore_signal(barrier, inc=1, device_id=partner, device_id_type=MESH)

    copies = {}

    def send(name, src, dst, target):
        number = IDS.names[name]
        copy = pltpu.make_async_remote_copy(
            src_ref=src, dst_ref=dst, send_sem=ssem.at[number], recv_sem=rsem.at[number],
            device_id=target, device_id_type=MESH)
        copy.start()
        copies[name] = copy

    def arrived(*name):
        copies[name].wait_recv()

    loads = [
        pltpu.make_async_copy(k_ref, kin, lsem.at[0]),
        pltpu.make_async_copy(q_ref, qin, lsem.at[1]),
        pltpu.make_async_copy(pat_ref, mb.at[0, :, 0:256], lsem.at[2]),
        pltpu.make_async_copy(pos_ref, mb.at[0, :, 256:384], lsem.at[3]),
        pltpu.make_async_copy(cl_ref, clv, lsem.at[4]),
        pltpu.make_async_copy(lm_ref, lmv, lsem.at[5]),
    ]
    for load in loads:
        load.start()
    loads[0].wait()
    kf = kin[...].astype(F32)
    kn = (kf * lax.rsqrt(jnp.sum(kf * kf, axis=1, keepdims=True) + EPS)).astype(BF16)
    kb[0, 0] = kn[:32]
    kb[0, 1] = kn[32:]
    pl.semaphore_wait(barrier, len(partners))

    def g_half(k, j):
        return kb.at[unit_of(k) * 4 + j, 0]

    def send_g(k, j, source):
        send(("g", k, j), source, g_half(k, j), at_z(1 if k < 4 else -1))

    def send_f(k, source):
        send(("f", k), source, kb.at[unit_of(k) * 4], at_z(1 if k <= 4 else -1))

    def b_half(k, j):
        return kb.at[unit_of(k) * 4 + j, 1]

    for d in (1, 3, 2):
        send(("xa", d), kb.at[0, 0], kb.at[d, 0], at_x(d))
    send_f(1, kb.at[0])
    send_f(7, kb.at[0])
    loads[1].wait()
    xf = qin[...].astype(F32)
    qb[0] = (xf * lax.rsqrt(jnp.sum(xf * xf, axis=1, keepdims=True) + EPS)).astype(BF16)
    send(("q", 1), qb.at[0], qb.at[1], at_y(1))
    send(("q", 3), qb.at[0], qb.at[3], at_y(-1))
    for load in loads[2:]:
        load.wait()
    for j in (1, 3, 2):
        arrived("xa", j)
        send_g(1, j, kb.at[j, 0])
        send_g(7, j, kb.at[j, 0])
    for d in (1, 3, 2):
        send(("xb", d), kb.at[0, 1], kb.at[d, 1], at_x(d))
    spread = lax.broadcasted_iota(I32, (64, 256), 0) == lax.broadcasted_iota(I32, (64, 256), 1) % 64
    clx[0] = jnp.dot(jnp.broadcast_to(clv[...].astype(F32), (8, 64)).astype(BF16), spread.astype(F32).astype(BF16),
                     preferred_element_type=F32)[0:1].astype(I32)
    for d in (1, 2, 3):
        send(("meta", d), mb.at[0], mb.at[d], at_y(d))
        send(("cx", d), clx.at[0], clx.at[d], at_x(d))

    def cluster_rows():
        for d in (1, 2, 3):
            arrived("cx", d)
        lane = lax.broadcasted_iota(I32, (1, 256), 1)
        row = clx[0]
        for d in (1, 2, 3):
            row = jnp.where(lane // 64 == d, clx[d], row)
        clz[0, 0] = row
        for k in range(1, 8):
            send(("cz", k), clz.at[0, 0], clz.at[0, k], at_z(k))

    def whole(k):
        arrived("f", k)
        if k < 4:
            send_f(k + 1, kb.at[unit_of(k) * 4])
        elif k > 5:
            send_f(k - 1, kb.at[unit_of(k) * 4])
        for d in (1, 3, 2):
            send(("bx", k, d), b_half(k, 0), b_half(k, d), at_x(d))

    def half(k, j):
        arrived("g", k, j)
        if k < 3:
            send_g(k + 1, j, g_half(k, j))
        elif k > 4:
            send_g(k - 1, j, g_half(k, j))

    def events(r):
        ks = (r, 8 - r) if r < 4 else (4,)
        steps = [functools.partial(whole, k) for k in ks]
        return steps + [functools.partial(half, k, j) for j in (1, 3, 2) for k in ks]

    def share(r):
        for k in (r, 8 - r) if 0 < r < 4 else (r,):
            for d in (1, 3, 2):
                if k:
                    arrived("bx", k, d)
                else:
                    arrived("xb", d)
            send(("sib", k), kb.at[pl.ds(unit_of(k) * 4, 4)], kb.at[pl.ds(sibling_unit(k) * 4, 4)], sibling)

    def queries_on():
        arrived("q", 1)
        send(("q2", 1), qb.at[1, 0:64], qb.at[2, 0:64], at_y(1))
        arrived("q", 3)
        send(("q2", 3), qb.at[3, 64:128], qb.at[2, 64:128], at_y(-1))

    def prepare():
        for k in range(1, 8):
            arrived("cz", k)
        send(("cs",), clz.at[0], clz.at[1], sibling)
        pm[...] = jnp.zeros_like(pm)
        for d in range(4):
            if d:
                arrived("meta", d)
            pm[d:d + 1, :] = mb[d, :, 0:256].astype(F32)
            pos = jnp.broadcast_to(mb[d, :, 256:384].astype(F32), (128, 128))
            pos_t[d * 128:(d + 1) * 128, :] = pos.T
        tot[...] = jnp.zeros_like(tot)
        pss[...] = jnp.zeros_like(pss)
        arrived("cs")
        arrived("q2", 1)
        arrived("q2", 3)

    def score(r, t, s, k):
        if s == 1:
            arrived("sib", k)
        unit = unit_of(r) + t
        keys = kb[unit * 4:unit * 4 + 4].reshape(256, 1024)
        sbuf[...] = lax.dot_general(qb[...].reshape(512, 1024), keys, (((1,), (1,)), ((), ())),
                                    preferred_element_type=F32)
        lanes = lax.broadcasted_iota(I32, (1, 256), 1)
        xx = (x - lanes // 64 + NX) % NX
        zz = (z - k + NZ) % NZ
        cc = c + s - 2 * c * s
        rank = (((xx % 2) * NY + y) * 2 + cc) * 16 + zz * 2 + xx // 2
        key_id = (rank * 64 + lanes % 64).astype(F32)
        hot = (lax.broadcasted_iota(I32, (256, 256), 0) == clz[s, k]).astype(F32).astype(BF16)
        amb[...] = lax.dot_general(pm[...].astype(BF16), hot, (((1,), (0,)), ((), ())),
                                   preferred_element_type=F32)
        for b in range(4):
            rows = slice(b * 128, (b + 1) * 128)
            for h in range(2):
                cols = slice(h * 128, (h + 1) * 128)
                st = sbuf[rows, cols]
                is_pos = pos_t[rows, :] == key_id[:, cols]
                one = jnp.where(is_pos, 1.0, 0.0)
                w = jnp.exp2(st * EXP2_SCALE) * jnp.maximum(one, amb[b:b + 1, cols])
                tot[rows, :] += w
                pss[rows, :] += st * one
                to = slice(t * 256 + h * 128, t * 256 + h * 128 + 128)
                wbuf[rows, to] = w.astype(BF16)
                obuf[rows, to] = one.astype(BF16)

    def column(r, units, n):
        first = unit_of(r)
        cols = slice(n * 256, (n + 1) * 256)
        keys = kb[first * 4:(first + units) * 4, :, :, cols].reshape(units * 256, 256)
        e_new = jnp.dot(wbuf[:, 0:units * 256], keys, preferred_element_type=F32)
        p_new = jnp.dot(obuf[:, 0:units * 256], keys, preferred_element_type=F32)
        if r == 0:
            e_acc[:, cols] = e_new
            p_acc[:, cols] = p_new
        else:
            e_acc[:, cols] += e_new
            p_acc[:, cols] += p_new

    def pieces(r):
        ks = (r, 8 - r) if 0 < r < 4 else (r,)
        order = [(s, k) for s in (0, 1) for k in ks]
        steps = [functools.partial(score, r, t, s, k) for t, (s, k) in enumerate(order)]
        return steps + [functools.partial(column, r, len(order), n) for n in range(4)]

    def run(first, second=()):
        first, second = list(first), list(second)
        done = 0
        for i, step in enumerate(first):
            step()
            upto = (i + 1) * len(second) // len(first)
            for other in second[done:upto]:
                other()
            done = upto

    steps = events(1)
    run(steps[:4])
    cluster_rows()
    queries_on()
    run(steps[4:])
    share(0)
    prepare()
    run(events(2), pieces(0))
    share(1)
    run(events(3), pieces(1))
    share(2)
    run(events(4), pieces(2))
    share(3)
    share(4)
    run(pieces(3))
    run(pieces(4))

    for b in range(4):
        rows = slice(b * 128, (b + 1) * 128)
        tb[0, b:b + 1, :] = jnp.sum(tot[rows, :].T, axis=0, keepdims=True)
        tb[0, 4 + b:5 + b, :] = jnp.sum(pss[rows, :].T, axis=0, keepdims=True)
    for d in (2, 1, 3):
        send(("tot", d), tb.at[0], tb.at[d], at_y(d))
    for d in (1, 3, 2):
        arrived("tot", d)

    def total_row(b, base):
        row = tb[0, base + b:base + b + 1, :]
        for d in (1, 2, 3):
            i = base + (b - d) % 4
            row = row + tb[d, i:i + 1, :]
        return row

    def partial_rows(b):
        inverse = (1.0 / jnp.broadcast_to(total_row(b, 0), (128, 128)).T)[:, 0:1]
        rows = slice(b * 128, (b + 1) * 128)
        return e_acc[rows, :] * inverse - p_acc[rows, :]

    for b in (2, 1, 3):
        pb[b - 1] = partial_rows(b).astype(BF16)
        send(("out", b), pb.at[b - 1], rb.at[b - 1], at_y(-b))
    ol_ref[...] = jnp.log(total_row(0, 0)) - total_row(0, 4) * 10.0
    og_ref[...] = partial_rows(0)
    for b in (1, 3, 2):
        arrived("out", b)
    direction = og_ref[...] + ((rb[0].astype(F32) + rb[1].astype(F32)) + rb[2].astype(F32))
    scale = (jnp.broadcast_to(lmv[...], (128, 128)).T)[:, 0:1] * 10.0
    xf = qin[...].astype(F32)
    q_scale = lax.rsqrt(jnp.sum(xf * xf, axis=1, keepdims=True) + EPS)
    g = direction * scale
    projection = jnp.sum(xf * g, axis=1, keepdims=True)
    og_ref[...] = q_scale * g - (q_scale * q_scale * q_scale * projection) * xf
    for copy in copies.values():
        copy.wait_send()


def body(queries, keys, pattern, clusters, positives, loss_multiplier):
    hbm = pl.BlockSpec(memory_space=pltpu.HBM)
    vmem = pl.BlockSpec(memory_space=pltpu.VMEM)
    count = len(IDS.names)
    grad, loss = pl.pallas_call(
        kernel,
        out_shape=(jax.ShapeDtypeStruct((128, 1024), F32), jax.ShapeDtypeStruct((1, 128), F32)),
        in_specs=[hbm] * 6,
        out_specs=(vmem, vmem),
        scratch_shapes=[
            pltpu.VMEM((64, 1024), BF16),
            pltpu.VMEM((128, 1024), BF16),
            pltpu.VMEM((1, 64), I32),
            pltpu.VMEM((1, 128), F32),
            pltpu.VMEM((64, 2, 32, 1024), BF16),
            pltpu.VMEM((4, 128, 1024), BF16),
            pltpu.VMEM((4, 1, 384), I32),
            pltpu.VMEM((4, 1, 256), I32),
            pltpu.VMEM((2, 8, 1, 256), I32),
            pltpu.VMEM((8, 256), F32),
            pltpu.VMEM((8, 256), F32),
            pltpu.VMEM((512, 1024), BF16),
            pltpu.VMEM((512, 1024), BF16),
            pltpu.VMEM((512, 256), F32),
            pltpu.VMEM((512, 1024), F32),
            pltpu.VMEM((512, 1024), F32),
            pltpu.VMEM((512, 128), F32),
            pltpu.VMEM((512, 128), F32),
            pltpu.VMEM((512, 128), F32),
            pltpu.VMEM((4, 8, 128), F32),
            pltpu.VMEM((3, 128, 1024), BF16),
            pltpu.VMEM((3, 128, 1024), BF16),
            pltpu.SemaphoreType.DMA((6,)),
            pltpu.SemaphoreType.DMA((count,)),
            pltpu.SemaphoreType.DMA((count,)),
        ],
        compiler_params=pltpu.CompilerParams(
            collective_id=0, has_side_effects=True, vmem_limit_bytes=63 * 1024 * 1024 + 768 * 1024),
        name="contrastive",
    )(queries, keys, pattern, clusters.reshape(1, 64), positives.reshape(1, 128), loss_multiplier.reshape(1, 128))
    return grad, loss.reshape(128)


def solution(mesh):
    rows, flat = P(("dp", "index"), None), P(("dp", "index"))
    return jax.shard_map(
        body, mesh=mesh, in_specs=(rows, rows, rows, flat, flat, flat), out_specs=(rows, flat), check_vma=False)
```

```python
import functools
import math

import jax
import jax.numpy as jnp
from jax import lax
from jax.experimental import pallas as pl
from jax.experimental.pallas import tpu as pltpu
from jax.sharding import PartitionSpec as P

MESH = pl.DeviceIdType.MESH
EPS = 1e-06
NX, NY, NZ = 4, 4, 8
EXP2_SCALE = 10.0 * math.log2(math.e)
F32, BF16, I32 = jnp.float32, jnp.bfloat16, jnp.int32


def unit_of(k):
    if k == 0:
        return 0
    if k == 4:
        return 14
    return 2 + 4 * (k - 1) if k < 4 else 2 + 4 * (7 - k) + 1


def sibling_unit(k):
    return unit_of(k) + (1 if k in (0, 4) else 2)


class Ids:
    def __init__(self):
        self.names = {}

    def __call__(self, *name):
        return self.names.setdefault(name, len(self.names))


def message_names():
    ids = Ids()
    for d in (1, 2, 3):
        ids("xa", d), ids("xb", d), ids("cx", d), ids("meta", d), ids("tot", d)
    for name in (("q", 1), ("q", 3), ("q2", 1), ("q2", 3), ("cs",)):
        ids(*name)
    for k in range(1, 8):
        ids("cz", k), ids("f", k)
        for d in (1, 2, 3):
            ids("bx", k, d), ids("g", k, d)
    for k in range(8):
        ids("sib", k)
    for n in range(4):
        for h in (0, 1):
            ids("rel", n, h), ids("out", 1, n, h), ids("out", 3, n, h)
    return ids


IDS = message_names()
STAGES = (((0,),), ((1, 7),), ((2, 6),), ((3, 5),), ((4,),))


def kernel(q_ref, k_ref, pat_ref, cl_ref, pos_ref, lm_ref, og_ref, ol_ref, kin, qin, clv, lmv, kb, qb, mb, clx, clz,
           pm, amb, wbuf, obuf, sbuf, e_acc, p_acc, pos_t, tot, pss, tb, pb, rb, rl, lsem, ssem, rsem):
    dp, ix = lax.axis_index("dp"), lax.axis_index("index")
    c, y, x, z = dp % 2, (dp // 2) % NY, (ix % 2) * 2 + dp // (2 * NY), ix // 2

    def dev(xx, yy, zz, cc):
        return ((xx % 2) * NY + yy) * 2 + cc, zz * 2 + xx // 2

    def at_x(d):
        return dev((x + d + NX) % NX, y, z, c)

    def at_y(d):
        return dev(x, (y + d + NY) % NY, z, c)

    def at_z(d):
        return dev(x, y, (z + d + NZ) % NZ, c)

    sibling = dev(x, y, z, 1 - c)
    partners = [at_x(d) for d in (1, 2, 3)] + [at_y(d) for d in (1, 2, 3)] + [at_z(d) for d in range(1, 8)] + [sibling]

    barrier = pltpu.get_barrier_semaphore()
    for partner in partners:
        pl.semaphore_signal(barrier, inc=1, device_id=partner, device_id_type=MESH)

    copies = {}

    def send(name, src, dst, target):
        number = IDS.names[name]
        copy = pltpu.make_async_remote_copy(
            src_ref=src, dst_ref=dst, send_sem=ssem.at[number], recv_sem=rsem.at[number],
            device_id=target, device_id_type=MESH)
        copy.start()
        copies[name] = copy

    def arrived(*name):
        copies[name].wait_recv()

    loads = [
        pltpu.make_async_copy(k_ref, kin, lsem.at[0]),
        pltpu.make_async_copy(q_ref, qin, lsem.at[1]),
        pltpu.make_async_copy(pat_ref, mb.at[0, :, 0:256], lsem.at[2]),
        pltpu.make_async_copy(pos_ref, mb.at[0, :, 256:384], lsem.at[3]),
        pltpu.make_async_copy(cl_ref, clv, lsem.at[4]),
        pltpu.make_async_copy(lm_ref, lmv, lsem.at[5]),
    ]
    for load in loads:
        load.start()
    for load in loads:
        load.wait()
    spread = lax.broadcasted_iota(I32, (64, 256), 0) == lax.broadcasted_iota(I32, (64, 256), 1) % 64
    clx[0] = jnp.dot(jnp.broadcast_to(clv[...].astype(F32), (8, 64)).astype(BF16), spread.astype(F32).astype(BF16),
                     preferred_element_type=F32)[0:1].astype(I32)
    kf = kin[...].astype(F32)
    kn = (kf * lax.rsqrt(jnp.sum(kf * kf, axis=1, keepdims=True) + EPS)).astype(BF16)
    kb[0, 0] = kn[:32]
    kb[0, 1] = kn[32:]
    xf = qin[...].astype(F32)
    qb[0] = (xf * lax.rsqrt(jnp.sum(xf * xf, axis=1, keepdims=True) + EPS)).astype(BF16)
    pl.semaphore_wait(barrier, len(partners))

    def g_half(k, j):
        return kb.at[unit_of(k) * 4 + j, 0]

    def send_g(k, j, source):
        send(("g", k, j), source, g_half(k, j), at_z(1 if k < 4 else -1))

    def send_f(k, source):
        send(("f", k), source, kb.at[unit_of(k) * 4], at_z(1 if k <= 4 else -1))

    def b_half(k, j):
        return kb.at[unit_of(k) * 4 + j, 1]

    for d in (1, 3, 2):
        send(("cx", d), clx.at[0], clx.at[d], at_x(d))
        send(("xa", d), kb.at[0, 0], kb.at[d, 0], at_x(d))
    send_f(1, kb.at[0])
    send_f(7, kb.at[0])
    send(("q", 1), qb.at[0], qb.at[1], at_y(1))
    send(("q", 3), qb.at[0], qb.at[3], at_y(-1))
    for d in (1, 2, 3):
        send(("meta", d), mb.at[0], mb.at[d], at_y(d))

    def near(j):
        arrived("xa", j)
        send_g(1, j, kb.at[j, 0])
        send_g(7, j, kb.at[j, 0])

    def cluster_rows():
        for d in (1, 2, 3):
            arrived("cx", d)
        lane = lax.broadcasted_iota(I32, (1, 256), 1)
        row = clx[0]
        for d in (1, 2, 3):
            row = jnp.where(lane // 64 == d, clx[d], row)
        clz[0, 0] = row
        for k in range(1, 8):
            send(("cz", k), clz.at[0, 0], clz.at[0, k], at_z(k))

    def whole(k):
        arrived("f", k)
        if k < 4:
            send_f(k + 1, kb.at[unit_of(k) * 4])
        elif k > 5:
            send_f(k - 1, kb.at[unit_of(k) * 4])
        for d in (1, 3, 2):
            send(("bx", k, d), b_half(k, 0), b_half(k, d), at_x(d))

    def half(k, j):
        arrived("g", k, j)
        if k < 3:
            send_g(k + 1, j, g_half(k, j))
        elif k > 4:
            send_g(k - 1, j, g_half(k, j))

    def share(r):
        for k in (r, 8 - r) if 0 < r < 4 else (r,):
            for d in (1, 3, 2):
                if k:
                    arrived("bx", k, d)
                else:
                    arrived("xb", d)
            send(("sib", k), kb.at[pl.ds(unit_of(k) * 4, 4)], kb.at[pl.ds(sibling_unit(k) * 4, 4)], sibling)

    def queries_on():
        arrived("q", 1)
        send(("q2", 1), qb.at[1, 0:64], qb.at[2, 0:64], at_y(1))
        arrived("q", 3)
        send(("q2", 3), qb.at[3, 64:128], qb.at[2, 64:128], at_y(-1))

    def prepare():
        for k in range(1, 8):
            arrived("cz", k)
        send(("cs",), clz.at[0], clz.at[1], sibling)
        pm[...] = jnp.zeros_like(pm)
        for d in range(4):
            if d:
                arrived("meta", d)
            pm[d:d + 1, :] = mb[d, :, 0:256].astype(F32)
            pos = jnp.broadcast_to(mb[d, :, 256:384].astype(F32), (128, 128))
            pos_t[d * 128:(d + 1) * 128, :] = pos.T
        tot[...] = jnp.zeros_like(tot)
        pss[...] = jnp.zeros_like(pss)
        arrived("cs")
        arrived("q2", 1)
        arrived("q2", 3)

    def score(first, t, s, k):
        if s == 1:
            arrived("sib", k)
        unit = first + t
        keys = kb[unit * 4:unit * 4 + 4].reshape(256, 1024)
        sbuf[...] = lax.dot_general(qb[...].reshape(512, 1024), keys, (((1,), (1,)), ((), ())),
                                    preferred_element_type=F32)
        lanes = lax.broadcasted_iota(I32, (1, 256), 1)
        xx = (x - lanes // 64 + NX) % NX
        zz = (z - k + NZ) % NZ
        cc = c + s - 2 * c * s
        rank = (((xx % 2) * NY + y) * 2 + cc) * 16 + zz * 2 + xx // 2
        key_id = (rank * 64 + lanes % 64).astype(F32)
        hot = (lax.broadcasted_iota(I32, (256, 256), 0) == clz[s, k]).astype(F32).astype(BF16)
        amb[...] = lax.dot_general(pm[...].astype(BF16), hot, (((1,), (0,)), ((), ())),
                                   preferred_element_type=F32)
        for b in range(4):
            rows = slice(b * 128, (b + 1) * 128)
            for h in range(2):
                cols = slice(h * 128, (h + 1) * 128)
                st = sbuf[rows, cols]
                is_pos = pos_t[rows, :] == key_id[:, cols]
                one = jnp.where(is_pos, 1.0, 0.0)
                w = jnp.exp2(st * EXP2_SCALE) * jnp.maximum(one, amb[b:b + 1, cols])
                tot[rows, :] += w
                pss[rows, :] += st * one
                to = slice(t * 256 + h * 128, t * 256 + h * 128 + 128)
                wbuf[rows, to] = w.astype(BF16)
                obuf[rows, to] = one.astype(BF16)

    def column(first, units, n):
        cols = slice(n * 256, (n + 1) * 256)
        keys = kb[first * 4:(first + units) * 4, :, :, cols].reshape(units * 256, 256)
        e_new = jnp.dot(wbuf[:, 0:units * 256], keys, preferred_element_type=F32)
        p_new = jnp.dot(obuf[:, 0:units * 256], keys, preferred_element_type=F32)
        if first == 0:
            e_acc[:, cols] = e_new
            p_acc[:, cols] = p_new
        else:
            e_acc[:, cols] += e_new
            p_acc[:, cols] += p_new

    def scores(stage):
        ks = STAGES[stage]
        steps = []
        for part in ks:
            for s in (0, 1):
                steps += [functools.partial(score, unit_of(ks[0][0]), len(steps) + i, s, k) for i, k in enumerate(part)]
        return steps

    def columns(stage):
        units = 2 * sum(len(part) for part in STAGES[stage])
        return [functools.partial(column, unit_of(STAGES[stage][0][0]), units, n) for n in range(4)]

    def run(first, second=()):
        first, second = list(first), list(second)
        done = 0
        for i, step in enumerate(first):
            step()
            upto = (i + 1) * len(second) // len(first)
            for other in second[done:upto]:
                other()
            done = upto

    def wholes(r):
        return [functools.partial(whole, k) for k in ((r, 8 - r) if r < 4 else (4,))]

    def halves(r, js=(1, 3, 2)):
        return [functools.partial(half, k, j) for j in js for k in ((r, 8 - r) if r < 4 else (4,))]

    def events(r):
        return wholes(r) + halves(r)

    cluster_rows()
    near(1)
    near(3)
    near(2)
    for d in (1, 3, 2):
        send(("xb", d), kb.at[0, 1], kb.at[d, 1], at_x(d))
    run(wholes(1) + halves(1, (1,)))
    queries_on()
    run(halves(1, (3, 2)))
    share(0)
    prepare()
    run(events(2), scores(0) + columns(0))
    share(1)
    run(events(3), scores(1) + columns(1))
    share(2)
    run(wholes(4), scores(2))
    run(halves(4, (1,)), columns(2))
    share(3)
    run(halves(4, (3, 2)), scores(3))
    share(4)
    run(columns(3))
    run(scores(4))

    for b in range(4):
        rows = slice(b * 128, (b + 1) * 128)
        tb[0, b:b + 1, :] = jnp.sum(tot[rows, :].T, axis=0, keepdims=True)
        tb[0, 4 + b:5 + b, :] = jnp.sum(pss[rows, :].T, axis=0, keepdims=True)
    for d in (2, 1, 3):
        send(("tot", d), tb.at[0], tb.at[d], at_y(d))

    def total_row(b, base):
        row = tb[0, base + b:base + b + 1, :]
        for d in (1, 2, 3):
            i = base + (b - d) % 4
            row = row + tb[d, i:i + 1, :]
        return row

    def partial_rows(b, cols):
        rows = slice(b * 128, (b + 1) * 128)
        inverse = jnp.concatenate([tot[rows, :]] * 2, axis=1)
        return e_acc[rows, cols] * inverse - p_acc[rows, cols]

    upper, lower = slice(0, 64), slice(64, 128)

    def leave(n):
        cols = slice(n * 256, (n + 1) * 256)
        pb[2, n] = partial_rows(2, cols).astype(BF16)
        send(("rel", n, 0), pb.at[2, n, upper], rl.at[0, n], at_y(-1))
        send(("rel", n, 1), pb.at[2, n, lower], rl.at[1, n], at_y(1))
        near_y = partial_rows(1, cols)
        pb[0, n, lower] = near_y[lower].astype(BF16)
        send(("out", 1, n, 1), pb.at[0, n, lower], rb.at[0, n, lower], at_y(-1))
        far_y = partial_rows(3, cols)
        pb[1, n, upper] = far_y[upper].astype(BF16)
        send(("out", 3, n, 0), pb.at[1, n, upper], rb.at[1, n, upper], at_y(1))

    def pass_on(n):
        cols = slice(n * 256, (n + 1) * 256)
        arrived("rel", n, 0)
        pb[0, n, upper] = (partial_rows(1, cols)[upper] + rl[0, n].astype(F32)).astype(BF16)
        send(("out", 1, n, 0), pb.at[0, n, upper], rb.at[0, n, upper], at_y(-1))
        arrived("rel", n, 1)
        pb[1, n, lower] = (partial_rows(3, cols)[lower] + rl[1, n].astype(F32)).astype(BF16)
        send(("out", 3, n, 1), pb.at[1, n, lower], rb.at[1, n, lower], at_y(1))

    final = columns(4)
    run(final[:2])
    for d in (1, 3, 2):
        arrived("tot", d)
    for b in (2, 1, 3, 0):
        tot[b * 128:(b + 1) * 128, :] = (1.0 / jnp.broadcast_to(total_row(b, 0), (128, 128))).T
    leave(0)
    leave(1)
    final[2]()
    leave(2)
    pass_on(0)
    final[3]()
    leave(3)
    pass_on(1)
    pass_on(2)
    pass_on(3)
    ol_ref[...] = jnp.log(total_row(0, 0)) - total_row(0, 4) * 10.0
    scale = (jnp.broadcast_to(lmv[...], (128, 128)).T)[:, 0:1] * 10.0
    projection = jnp.zeros((128, 1), F32)
    for n in range(4):
        cols = slice(n * 256, (n + 1) * 256)
        for b in (1, 3):
            for h in (0, 1):
                arrived("out", b, n, h)
        direction = partial_rows(0, cols) + (rb[0, n].astype(F32) + rb[1, n].astype(F32))
        g = direction * scale
        og_ref[:, cols] = g
        projection = projection + jnp.sum(qin[:, cols].astype(F32) * g, axis=1, keepdims=True)
    xf = qin[...].astype(F32)
    q_scale = lax.rsqrt(jnp.sum(xf * xf, axis=1, keepdims=True) + EPS)
    og_ref[...] = q_scale * og_ref[...] - (q_scale * q_scale * q_scale * projection) * xf
    for copy in copies.values():
        copy.wait_send()


def body(queries, keys, pattern, clusters, positives, loss_multiplier):
    hbm = pl.BlockSpec(memory_space=pltpu.HBM)
    vmem = pl.BlockSpec(memory_space=pltpu.VMEM)
    count = len(IDS.names)
    grad, loss = pl.pallas_call(
        kernel,
        out_shape=(jax.ShapeDtypeStruct((128, 1024), F32), jax.ShapeDtypeStruct((1, 128), F32)),
        in_specs=[hbm] * 6,
        out_specs=(vmem, vmem),
        scratch_shapes=[
            pltpu.VMEM((64, 1024), BF16),
            pltpu.VMEM((128, 1024), BF16),
            pltpu.VMEM((1, 64), I32),
            pltpu.VMEM((1, 128), F32),
            pltpu.VMEM((64, 2, 32, 1024), BF16),
            pltpu.VMEM((4, 128, 1024), BF16),
            pltpu.VMEM((4, 1, 384), I32),
            pltpu.VMEM((4, 1, 256), I32),
            pltpu.VMEM((2, 8, 1, 256), I32),
            pltpu.VMEM((8, 256), F32),
            pltpu.VMEM((8, 256), F32),
            pltpu.VMEM((512, 1024), BF16),
            pltpu.VMEM((512, 1024), BF16),
            pltpu.VMEM((512, 256), F32),
            pltpu.VMEM((512, 1024), F32),
            pltpu.VMEM((512, 1024), F32),
            pltpu.VMEM((512, 128), F32),
            pltpu.VMEM((512, 128), F32),
            pltpu.VMEM((512, 128), F32),
            pltpu.VMEM((4, 8, 128), F32),
            pltpu.VMEM((3, 4, 128, 256), BF16),
            pltpu.VMEM((2, 4, 128, 256), BF16),
            pltpu.VMEM((2, 4, 64, 256), BF16),
            pltpu.SemaphoreType.DMA((6,)),
            pltpu.SemaphoreType.DMA((count,)),
            pltpu.SemaphoreType.DMA((count,)),
        ],
        compiler_params=pltpu.CompilerParams(
            collective_id=0, has_side_effects=True, vmem_limit_bytes=63 * 1024 * 1024 + 768 * 1024),
        name="contrastive",
    )(queries, keys, pattern, clusters.reshape(1, 64), positives.reshape(1, 128), loss_multiplier.reshape(1, 128))
    return grad, loss.reshape(128)


def solution(mesh):
    rows, flat = P(("dp", "index"), None), P(("dp", "index"))
    return jax.shard_map(
        body, mesh=mesh, in_specs=(rows, rows, rows, flat, flat, flat), out_specs=(rows, flat), check_vma=False)
```

```python
import functools
import math

import jax
import jax.numpy as jnp
from jax import lax
from jax.experimental import pallas as pl
from jax.experimental.pallas import tpu as pltpu
from jax.sharding import PartitionSpec as P

MESH = pl.DeviceIdType.MESH
EPS = 1e-06
NX, NY, NZ = 4, 4, 8
EXP2_SCALE = 10.0 * math.log2(math.e)
F32, BF16, I32 = jnp.float32, jnp.bfloat16, jnp.int32


def unit_of(k):
    if k == 0:
        return 0
    if k == 4:
        return 14
    return 2 + 4 * (k - 1) if k < 4 else 2 + 4 * (7 - k) + 1


def sibling_unit(k):
    return unit_of(k) + (1 if k in (0, 4) else 2)


class Ids:
    def __init__(self):
        self.names = {}

    def __call__(self, *name):
        return self.names.setdefault(name, len(self.names))


def message_names():
    ids = Ids()
    for d in (1, 2, 3):
        ids("xa", d), ids("xb", d), ids("cx", d), ids("meta", d), ids("tot", d)
    for name in (("q", 1), ("q", 3), ("q2", 1), ("q2", 3), ("cs",)):
        ids(*name)
    for k in range(1, 8):
        ids("cz", k), ids("f", k)
        for d in (1, 2, 3):
            ids("bx", k, d), ids("g", k, d)
    for k in range(8):
        if k != 4:
            ids("sib", k)
    ids("sw"), ids("sg", 0), ids("sg", 1), ids("sg", 2), ids("sg", 3)
    for n in range(4):
        for h in (0, 1):
            ids("rel", n, h), ids("out", 1, n, h), ids("out", 3, n, h)
    return ids


IDS = message_names()
STAGES = (((0,),), ((1, 7),), ((2, 6),), ((3, 5), (4,)))


def kernel(q_ref, k_ref, pat_ref, cl_ref, pos_ref, lm_ref, og_ref, ol_ref, kin, qin, clv, lmv, kb, qb, mb, clx, clz,
           pm, amb, wbuf, obuf, sbuf, e_acc, p_acc, pos_t, tot, pss, tb, pb, rb, rl, lsem, ssem, rsem):
    dp, ix = lax.axis_index("dp"), lax.axis_index("index")
    c, y, x, z = dp % 2, (dp // 2) % NY, (ix % 2) * 2 + dp // (2 * NY), ix // 2

    def dev(xx, yy, zz, cc):
        return ((xx % 2) * NY + yy) * 2 + cc, zz * 2 + xx // 2

    def at_x(d):
        return dev((x + d + NX) % NX, y, z, c)

    def at_y(d):
        return dev(x, (y + d + NY) % NY, z, c)

    def at_z(d):
        return dev(x, y, (z + d + NZ) % NZ, c)

    sibling = dev(x, y, z, 1 - c)
    partners = [at_x(d) for d in (1, 2, 3)] + [at_y(d) for d in (1, 2, 3)] + [at_z(d) for d in range(1, 8)] + [sibling]

    barrier = pltpu.get_barrier_semaphore()
    for partner in partners:
        pl.semaphore_signal(barrier, inc=1, device_id=partner, device_id_type=MESH)

    copies = {}

    def send(name, src, dst, target):
        number = IDS.names[name]
        copy = pltpu.make_async_remote_copy(
            src_ref=src, dst_ref=dst, send_sem=ssem.at[number], recv_sem=rsem.at[number],
            device_id=target, device_id_type=MESH)
        copy.start()
        copies[name] = copy

    def arrived(*name):
        copies[name].wait_recv()

    loads = [
        pltpu.make_async_copy(k_ref, kin, lsem.at[0]),
        pltpu.make_async_copy(q_ref, qin, lsem.at[1]),
        pltpu.make_async_copy(pat_ref, mb.at[0, :, 0:256], lsem.at[2]),
        pltpu.make_async_copy(pos_ref, mb.at[0, :, 256:384], lsem.at[3]),
        pltpu.make_async_copy(cl_ref, clv, lsem.at[4]),
        pltpu.make_async_copy(lm_ref, lmv, lsem.at[5]),
    ]
    for load in loads:
        load.start()
    for load in loads:
        load.wait()
    spread = lax.broadcasted_iota(I32, (64, 256), 0) == lax.broadcasted_iota(I32, (64, 256), 1) % 64
    clx[0] = jnp.dot(jnp.broadcast_to(clv[...].astype(F32), (8, 64)).astype(BF16), spread.astype(F32).astype(BF16),
                     preferred_element_type=F32)[0:1].astype(I32)
    kf = kin[...].astype(F32)
    kn = (kf * lax.rsqrt(jnp.sum(kf * kf, axis=1, keepdims=True) + EPS)).astype(BF16)
    kb[0, 0] = kn[:32]
    kb[0, 1] = kn[32:]
    xf = qin[...].astype(F32)
    qb[0] = (xf * lax.rsqrt(jnp.sum(xf * xf, axis=1, keepdims=True) + EPS)).astype(BF16)
    pl.semaphore_wait(barrier, len(partners))

    def g_half(k, j):
        return kb.at[unit_of(k) * 4 + j, 0]

    def send_g(k, j, source):
        send(("g", k, j), source, g_half(k, j), at_z(1 if k < 4 else -1))

    def send_f(k, source):
        send(("f", k), source, kb.at[unit_of(k) * 4], at_z(1 if k <= 4 else -1))

    def b_half(k, j):
        return kb.at[unit_of(k) * 4 + j, 1]

    for d in (1, 3, 2):
        send(("cx", d), clx.at[0], clx.at[d], at_x(d))
        send(("xa", d), kb.at[0, 0], kb.at[d, 0], at_x(d))
    send_f(1, kb.at[0])
    send_f(7, kb.at[0])
    send(("q", 1), qb.at[0], qb.at[1], at_y(1))
    send(("q", 3), qb.at[0], qb.at[3], at_y(-1))
    for d in (1, 2, 3):
        send(("meta", d), mb.at[0], mb.at[d], at_y(d))

    def near(j):
        arrived("xa", j)
        send_g(1, j, kb.at[j, 0])
        send_g(7, j, kb.at[j, 0])

    def cluster_rows():
        for d in (1, 2, 3):
            arrived("cx", d)
        lane = lax.broadcasted_iota(I32, (1, 256), 1)
        row = clx[0]
        for d in (1, 2, 3):
            row = jnp.where(lane // 64 == d, clx[d], row)
        clz[0, 0] = row
        for k in range(1, 8):
            send(("cz", k), clz.at[0, 0], clz.at[0, k], at_z(k))

    def whole(k):
        arrived("f", k)
        if k < 4:
            send_f(k + 1, kb.at[unit_of(k) * 4])
        elif k > 5:
            send_f(k - 1, kb.at[unit_of(k) * 4])
        for d in (1, 3, 2):
            send(("bx", k, d), b_half(k, 0), b_half(k, d), at_x(d))

    def to_sibling(j):
        u, v = unit_of(4) * 4 + j, sibling_unit(4) * 4 + j
        send(("sg", j), kb.at[u, 0], kb.at[v, 0], sibling)

    def half(k, j):
        arrived("g", k, j)
        if k == 4:
            to_sibling(j)
        if k < 3:
            send_g(k + 1, j, g_half(k, j))
        elif k > 4:
            send_g(k - 1, j, g_half(k, j))

    def share(r):
        for k in (r, 8 - r) if 0 < r < 4 else (r,):
            for d in (1, 3, 2):
                if k:
                    arrived("bx", k, d)
                else:
                    arrived("xb", d)
            if k == 4:
                to_sibling(0)
                u, v = unit_of(4) * 4, sibling_unit(4) * 4
                send(("sw",), kb.at[u:u + 4, 1], kb.at[v:v + 4, 1], sibling)
                continue
            send(("sib", k), kb.at[pl.ds(unit_of(k) * 4, 4)], kb.at[pl.ds(sibling_unit(k) * 4, 4)], sibling)

    def queries_on():
        arrived("q", 1)
        send(("q2", 1), qb.at[1, 0:64], qb.at[2, 0:64], at_y(1))
        arrived("q", 3)
        send(("q2", 3), qb.at[3, 64:128], qb.at[2, 64:128], at_y(-1))

    def prepare():
        for k in range(1, 8):
            arrived("cz", k)
        send(("cs",), clz.at[0], clz.at[1], sibling)
        pm[...] = jnp.zeros_like(pm)
        for d in range(4):
            if d:
                arrived("meta", d)
            pm[d:d + 1, :] = mb[d, :, 0:256].astype(F32)
            pos = jnp.broadcast_to(mb[d, :, 256:384].astype(F32), (128, 128))
            pos_t[d * 128:(d + 1) * 128, :] = pos.T
        tot[...] = jnp.zeros_like(tot)
        pss[...] = jnp.zeros_like(pss)
        arrived("cs")
        arrived("q2", 1)
        arrived("q2", 3)

    def score(first, t, s, k):
        if s == 1 and k == 4:
            arrived("sw")
            for j in range(4):
                arrived("sg", j)
        elif s == 1:
            arrived("sib", k)
        unit = first + t
        keys = kb[unit * 4:unit * 4 + 4].reshape(256, 1024)
        sbuf[...] = lax.dot_general(qb[...].reshape(512, 1024), keys, (((1,), (1,)), ((), ())),
                                    preferred_element_type=F32)
        lanes = lax.broadcasted_iota(I32, (1, 256), 1)
        xx = (x - lanes // 64 + NX) % NX
        zz = (z - k + NZ) % NZ
        cc = c + s - 2 * c * s
        rank = (((xx % 2) * NY + y) * 2 + cc) * 16 + zz * 2 + xx // 2
        key_id = (rank * 64 + lanes % 64).astype(F32)
        hot = (lax.broadcasted_iota(I32, (256, 256), 0) == clz[s, k]).astype(F32).astype(BF16)
        amb[...] = lax.dot_general(pm[...].astype(BF16), hot, (((1,), (0,)), ((), ())),
                                   preferred_element_type=F32)
        for b in range(4):
            rows = slice(b * 128, (b + 1) * 128)
            for h in range(2):
                cols = slice(h * 128, (h + 1) * 128)
                st = sbuf[rows, cols]
                is_pos = pos_t[rows, :] == key_id[:, cols]
                one = jnp.where(is_pos, 1.0, 0.0)
                w = jnp.exp2(st * EXP2_SCALE) * jnp.maximum(one, amb[b:b + 1, cols])
                tot[rows, :] += w
                pss[rows, :] += st * one
                to = slice(t * 256 + h * 128, t * 256 + h * 128 + 128)
                wbuf[rows, to] = w.astype(BF16)
                obuf[rows, to] = one.astype(BF16)

    def column(first, units, n):
        cols = slice(n * 256, (n + 1) * 256)
        keys = kb[first * 4:(first + units) * 4, :, :, cols].reshape(units * 256, 256)
        e_new = jnp.dot(wbuf[:, 0:units * 256], keys, preferred_element_type=F32)
        p_new = jnp.dot(obuf[:, 0:units * 256], keys, preferred_element_type=F32)
        if first == 0:
            e_acc[:, cols] = e_new
            p_acc[:, cols] = p_new
        else:
            e_acc[:, cols] += e_new
            p_acc[:, cols] += p_new

    def scores(stage):
        ks = STAGES[stage]
        steps = []
        for part in ks:
            for s in (0, 1):
                steps += [functools.partial(score, unit_of(ks[0][0]), len(steps) + i, s, k) for i, k in enumerate(part)]
        return steps

    def columns(stage):
        units = 2 * sum(len(part) for part in STAGES[stage])
        return [functools.partial(column, unit_of(STAGES[stage][0][0]), units, n) for n in range(4)]

    def run(first, second=()):
        first, second = list(first), list(second)
        done = 0
        for i, step in enumerate(first):
            step()
            upto = (i + 1) * len(second) // len(first)
            for other in second[done:upto]:
                other()
            done = upto

    def wholes(r):
        return [functools.partial(whole, k) for k in ((r, 8 - r) if r < 4 else (4,))]

    def halves(r, js=(1, 3, 2)):
        return [functools.partial(half, k, j) for j in js for k in ((r, 8 - r) if r < 4 else (4,))]

    def events(r):
        return wholes(r) + halves(r)

    cluster_rows()
    near(1)
    near(3)
    near(2)
    for d in (1, 3, 2):
        send(("xb", d), kb.at[0, 1], kb.at[d, 1], at_x(d))
    run(wholes(1) + halves(1, (1,)))
    queries_on()
    run(halves(1, (3, 2)))
    share(0)
    prepare()
    run(events(2), scores(0) + columns(0))
    share(1)
    run(events(3), scores(1) + columns(1))
    share(2)
    run(wholes(4), scores(2))
    run(halves(4, (1,)), columns(2))
    share(3)
    last = scores(3)
    run(halves(4, (3,)), last[:2])
    share(4)
    run(halves(4, (2,)), last[2:4])
    run(last[4:])

    for b in range(4):
        rows = slice(b * 128, (b + 1) * 128)
        tb[0, b:b + 1, :] = jnp.sum(tot[rows, :].T, axis=0, keepdims=True)
        tb[0, 4 + b:5 + b, :] = jnp.sum(pss[rows, :].T, axis=0, keepdims=True)
    for d in (2, 1, 3):
        send(("tot", d), tb.at[0], tb.at[d], at_y(d))

    def total_row(b, base):
        row = tb[0, base + b:base + b + 1, :]
        for d in (1, 2, 3):
            i = base + (b - d) % 4
            row = row + tb[d, i:i + 1, :]
        return row

    def partial_rows(b, cols):
        rows = slice(b * 128, (b + 1) * 128)
        inverse = jnp.concatenate([tot[rows, :]] * 2, axis=1)
        return e_acc[rows, cols] * inverse - p_acc[rows, cols]

    upper, lower = slice(0, 64), slice(64, 128)

    def leave(n):
        cols = slice(n * 256, (n + 1) * 256)
        pb[2, n] = partial_rows(2, cols).astype(BF16)
        send(("rel", n, 0), pb.at[2, n, upper], rl.at[0, n], at_y(-1))
        send(("rel", n, 1), pb.at[2, n, lower], rl.at[1, n], at_y(1))
        near_y = partial_rows(1, cols)
        pb[0, n, lower] = near_y[lower].astype(BF16)
        send(("out", 1, n, 1), pb.at[0, n, lower], rb.at[0, n, lower], at_y(-1))
        far_y = partial_rows(3, cols)
        pb[1, n, upper] = far_y[upper].astype(BF16)
        send(("out", 3, n, 0), pb.at[1, n, upper], rb.at[1, n, upper], at_y(1))

    def pass_on(n):
        cols = slice(n * 256, (n + 1) * 256)
        arrived("rel", n, 0)
        pb[0, n, upper] = (partial_rows(1, cols)[upper] + rl[0, n].astype(F32)).astype(BF16)
        send(("out", 1, n, 0), pb.at[0, n, upper], rb.at[0, n, upper], at_y(-1))
        arrived("rel", n, 1)
        pb[1, n, lower] = (partial_rows(3, cols)[lower] + rl[1, n].astype(F32)).astype(BF16)
        send(("out", 3, n, 1), pb.at[1, n, lower], rb.at[1, n, lower], at_y(1))

    final = columns(3)
    run(final[:2])
    for d in (1, 3, 2):
        arrived("tot", d)
    for b in (2, 1, 3, 0):
        tot[b * 128:(b + 1) * 128, :] = (1.0 / jnp.broadcast_to(total_row(b, 0), (128, 128))).T
    leave(0)
    leave(1)
    final[2]()
    leave(2)
    pass_on(0)
    final[3]()
    leave(3)
    pass_on(1)
    pass_on(2)
    pass_on(3)
    ol_ref[...] = jnp.log(total_row(0, 0)) - total_row(0, 4) * 10.0
    scale = (jnp.broadcast_to(lmv[...], (128, 128)).T)[:, 0:1] * 10.0
    projection = jnp.zeros((128, 1), F32)
    for n in range(4):
        cols = slice(n * 256, (n + 1) * 256)
        for b in (1, 3):
            for h in (0, 1):
                arrived("out", b, n, h)
        direction = partial_rows(0, cols) + (rb[0, n].astype(F32) + rb[1, n].astype(F32))
        g = direction * scale
        og_ref[:, cols] = g
        projection = projection + jnp.sum(qin[:, cols].astype(F32) * g, axis=1, keepdims=True)
    xf = qin[...].astype(F32)
    q_scale = lax.rsqrt(jnp.sum(xf * xf, axis=1, keepdims=True) + EPS)
    og_ref[...] = q_scale * og_ref[...] - (q_scale * q_scale * q_scale * projection) * xf
    for copy in copies.values():
        copy.wait_send()


def body(queries, keys, pattern, clusters, positives, loss_multiplier):
    hbm = pl.BlockSpec(memory_space=pltpu.HBM)
    vmem = pl.BlockSpec(memory_space=pltpu.VMEM)
    count = len(IDS.names)
    grad, loss = pl.pallas_call(
        kernel,
        out_shape=(jax.ShapeDtypeStruct((128, 1024), F32), jax.ShapeDtypeStruct((1, 128), F32)),
        in_specs=[hbm] * 6,
        out_specs=(vmem, vmem),
        scratch_shapes=[
            pltpu.VMEM((64, 1024), BF16),
            pltpu.VMEM((128, 1024), BF16),
            pltpu.VMEM((1, 64), I32),
            pltpu.VMEM((1, 128), F32),
            pltpu.VMEM((64, 2, 32, 1024), BF16),
            pltpu.VMEM((4, 128, 1024), BF16),
            pltpu.VMEM((4, 1, 384), I32),
            pltpu.VMEM((4, 1, 256), I32),
            pltpu.VMEM((2, 8, 1, 256), I32),
            pltpu.VMEM((8, 256), F32),
            pltpu.VMEM((8, 256), F32),
            pltpu.VMEM((512, 1536), BF16),
            pltpu.VMEM((512, 1536), BF16),
            pltpu.VMEM((512, 256), F32),
            pltpu.VMEM((512, 1024), F32),
            pltpu.VMEM((512, 1024), F32),
            pltpu.VMEM((512, 128), F32),
            pltpu.VMEM((512, 128), F32),
            pltpu.VMEM((512, 128), F32),
            pltpu.VMEM((4, 8, 128), F32),
            pltpu.VMEM((3, 4, 128, 256), BF16),
            pltpu.VMEM((2, 4, 128, 256), BF16),
            pltpu.VMEM((2, 4, 64, 256), BF16),
            pltpu.SemaphoreType.DMA((6,)),
            pltpu.SemaphoreType.DMA((count,)),
            pltpu.SemaphoreType.DMA((count,)),
        ],
        compiler_params=pltpu.CompilerParams(
            collective_id=0, has_side_effects=True, vmem_limit_bytes=63 * 1024 * 1024 + 768 * 1024),
        name="contrastive",
    )(queries, keys, pattern, clusters.reshape(1, 64), positives.reshape(1, 128), loss_multiplier.reshape(1, 128))
    return grad, loss.reshape(128)


def solution(mesh):
    rows, flat = P(("dp", "index"), None), P(("dp", "index"))
    return jax.shard_map(
        body, mesh=mesh, in_specs=(rows, rows, rows, flat, flat, flat), out_specs=(rows, flat), check_vma=False)
```

```python
import functools
import math

import jax
import jax.numpy as jnp
from jax import lax
from jax.experimental import pallas as pl
from jax.experimental.pallas import tpu as pltpu
from jax.sharding import PartitionSpec as P

MESH = pl.DeviceIdType.MESH
EPS = 1e-06
NX, NY, NZ = 4, 4, 8
EXP2_SCALE = 10.0 * math.log2(math.e)
F32, BF16, I32 = jnp.float32, jnp.bfloat16, jnp.int32


def unit_of(k):
    if k == 0:
        return 0
    if k == 4:
        return 14
    return 2 + 4 * (k - 1) if k < 4 else 2 + 4 * (7 - k) + 1


def sibling_unit(k):
    return unit_of(k) + (1 if k in (0, 4) else 2)


class Ids:
    def __init__(self):
        self.names = {}

    def __call__(self, *name):
        return self.names.setdefault(name, len(self.names))


def message_names():
    ids = Ids()
    for d in (1, 2, 3):
        ids("xa", d), ids("xb", d), ids("cx", d), ids("meta", d), ids("tot", d), ids("ps", d)
    for name in (("q", 1), ("q", 3), ("q2", 1), ("q2", 3), ("cs",)):
        ids(*name)
    for k in range(1, 8):
        ids("cz", k), ids("f", k)
        for d in (1, 2, 3):
            ids("bx", k, d), ids("g", k, d)
    for k in range(8):
        if k != 4:
            ids("sib", k)
    ids("sw"), ids("sg", 0), ids("sg", 1), ids("sg", 2), ids("sg", 3)
    for n in range(4):
        for h in (0, 1):
            ids("rel", n, h), ids("out", 1, n, h), ids("out", 3, n, h)
    return ids


IDS = message_names()
STAGES = (((0,),), ((1, 7),), ((2, 6),), ((3, 5), (4,)))


def kernel(q_ref, k_ref, pat_ref, cl_ref, pos_ref, lm_ref, og_ref, ol_ref, kin, qin, clv, lmv, kb, qb, mb, clx, clz,
           pm, amb, wbuf, obuf, sbuf, e_acc, p_acc, pos_t, tot, pss, tb, pb, rb, rl, lsem, ssem, rsem):
    dp, ix = lax.axis_index("dp"), lax.axis_index("index")
    c, y, x, z = dp % 2, (dp // 2) % NY, (ix % 2) * 2 + dp // (2 * NY), ix // 2

    def dev(xx, yy, zz, cc):
        return ((xx % 2) * NY + yy) * 2 + cc, zz * 2 + xx // 2

    def at_x(d):
        return dev((x + d + NX) % NX, y, z, c)

    def at_y(d):
        return dev(x, (y + d + NY) % NY, z, c)

    def at_z(d):
        return dev(x, y, (z + d + NZ) % NZ, c)

    sibling = dev(x, y, z, 1 - c)
    partners = [at_x(d) for d in (1, 2, 3)] + [at_y(d) for d in (1, 2, 3)] + [at_z(d) for d in range(1, 8)] + [sibling]

    barrier = pltpu.get_barrier_semaphore()
    for partner in partners:
        pl.semaphore_signal(barrier, inc=1, device_id=partner, device_id_type=MESH)

    copies = {}

    def send(name, src, dst, target):
        number = IDS.names[name]
        copy = pltpu.make_async_remote_copy(
            src_ref=src, dst_ref=dst, send_sem=ssem.at[number], recv_sem=rsem.at[number],
            device_id=target, device_id_type=MESH)
        copy.start()
        copies[name] = copy

    def arrived(*name):
        copies[name].wait_recv()

    loads = [
        pltpu.make_async_copy(k_ref, kin, lsem.at[0]),
        pltpu.make_async_copy(q_ref, qin, lsem.at[1]),
        pltpu.make_async_copy(pat_ref, mb.at[0, :, 0:256], lsem.at[2]),
        pltpu.make_async_copy(pos_ref, mb.at[0, :, 256:384], lsem.at[3]),
        pltpu.make_async_copy(cl_ref, clv, lsem.at[4]),
        pltpu.make_async_copy(lm_ref, lmv, lsem.at[5]),
    ]
    for load in loads:
        load.start()
    for load in loads:
        load.wait()
    spread = lax.broadcasted_iota(I32, (64, 256), 0) == lax.broadcasted_iota(I32, (64, 256), 1) % 64
    clx[0] = jnp.dot(jnp.broadcast_to(clv[...].astype(F32), (8, 64)).astype(BF16), spread.astype(F32).astype(BF16),
                     preferred_element_type=F32)[0:1].astype(I32)
    kf = kin[...].astype(F32)
    kn = (kf * lax.rsqrt(jnp.sum(kf * kf, axis=1, keepdims=True) + EPS)).astype(BF16)
    kb[0, 0] = kn[:32]
    kb[0, 1] = kn[32:]
    xf = qin[...].astype(F32)
    qb[0] = (xf * lax.rsqrt(jnp.sum(xf * xf, axis=1, keepdims=True) + EPS)).astype(BF16)
    pl.semaphore_wait(barrier, len(partners))

    def g_half(k, j):
        return kb.at[unit_of(k) * 4 + j, 0]

    def send_g(k, j, source):
        send(("g", k, j), source, g_half(k, j), at_z(1 if k < 4 else -1))

    def send_f(k, source):
        send(("f", k), source, kb.at[unit_of(k) * 4], at_z(1 if k <= 4 else -1))

    def b_half(k, j):
        return kb.at[unit_of(k) * 4 + j, 1]

    for d in (1, 3, 2):
        send(("cx", d), clx.at[0], clx.at[d], at_x(d))
        send(("xa", d), kb.at[0, 0], kb.at[d, 0], at_x(d))
    send_f(1, kb.at[0])
    send_f(7, kb.at[0])
    send(("q", 1), qb.at[0], qb.at[1], at_y(1))
    send(("q", 3), qb.at[0], qb.at[3], at_y(-1))
    for d in (1, 2, 3):
        send(("meta", d), mb.at[0], mb.at[d], at_y(d))

    def near(j):
        arrived("xa", j)
        send_g(1, j, kb.at[j, 0])
        send_g(7, j, kb.at[j, 0])

    def cluster_rows():
        for d in (1, 2, 3):
            arrived("cx", d)
        lane = lax.broadcasted_iota(I32, (1, 256), 1)
        row = clx[0]
        for d in (1, 2, 3):
            row = jnp.where(lane // 64 == d, clx[d], row)
        clz[0, 0] = row
        for k in range(1, 8):
            send(("cz", k), clz.at[0, 0], clz.at[0, k], at_z(k))

    def whole(k):
        arrived("f", k)
        if k < 4:
            send_f(k + 1, kb.at[unit_of(k) * 4])
        elif k > 5:
            send_f(k - 1, kb.at[unit_of(k) * 4])
        for d in (1, 3, 2):
            send(("bx", k, d), b_half(k, 0), b_half(k, d), at_x(d))

    def to_sibling(j):
        u, v = unit_of(4) * 4 + j, sibling_unit(4) * 4 + j
        send(("sg", j), kb.at[u, 0], kb.at[v, 0], sibling)

    def half(k, j):
        arrived("g", k, j)
        if k == 4:
            to_sibling(j)
        if k < 3:
            send_g(k + 1, j, g_half(k, j))
        elif k > 4:
            send_g(k - 1, j, g_half(k, j))

    def share(r):
        for k in (r, 8 - r) if 0 < r < 4 else (r,):
            for d in (1, 3, 2):
                if k:
                    arrived("bx", k, d)
                else:
                    arrived("xb", d)
            if k == 4:
                to_sibling(0)
                u, v = unit_of(4) * 4, sibling_unit(4) * 4
                send(("sw",), kb.at[u:u + 4, 1], kb.at[v:v + 4, 1], sibling)
                continue
            send(("sib", k), kb.at[pl.ds(unit_of(k) * 4, 4)], kb.at[pl.ds(sibling_unit(k) * 4, 4)], sibling)

    def queries_on():
        arrived("q", 1)
        send(("q2", 1), qb.at[1, 0:64], qb.at[2, 0:64], at_y(1))
        arrived("q", 3)
        send(("q2", 3), qb.at[3, 64:128], qb.at[2, 64:128], at_y(-1))

    def prepare():
        for k in range(1, 8):
            arrived("cz", k)
        send(("cs",), clz.at[0], clz.at[1], sibling)
        pm[...] = jnp.zeros_like(pm)
        for d in range(4):
            if d:
                arrived("meta", d)
            pm[d:d + 1, :] = mb[d, :, 0:256].astype(F32)
            pos = jnp.broadcast_to(mb[d, :, 256:384].astype(F32), (128, 128))
            pos_t[d * 128:(d + 1) * 128, :] = pos.T
        tot[...] = jnp.zeros_like(tot)
        pss[...] = jnp.zeros_like(pss)
        arrived("cs")
        arrived("q2", 1)
        arrived("q2", 3)

    def score(first, t, s, k):
        if s == 1 and k == 4:
            arrived("sw")
            for j in range(4):
                arrived("sg", j)
        elif s == 1:
            arrived("sib", k)
        unit = first + t
        keys = kb[unit * 4:unit * 4 + 4].reshape(256, 1024)
        sbuf[...] = lax.dot_general(qb[...].reshape(512, 1024), keys, (((1,), (1,)), ((), ())),
                                    preferred_element_type=F32)
        lanes = lax.broadcasted_iota(I32, (1, 256), 1)
        xx = (x - lanes // 64 + NX) % NX
        zz = (z - k + NZ) % NZ
        cc = c + s - 2 * c * s
        rank = (((xx % 2) * NY + y) * 2 + cc) * 16 + zz * 2 + xx // 2
        key_id = (rank * 64 + lanes % 64).astype(F32)
        hot = (lax.broadcasted_iota(I32, (256, 256), 0) == clz[s, k]).astype(F32).astype(BF16)
        amb[...] = lax.dot_general(pm[...].astype(BF16), hot, (((1,), (0,)), ((), ())),
                                   preferred_element_type=F32)
        for b in range(4):
            rows = slice(b * 128, (b + 1) * 128)
            sums, picked = [], []
            for h in range(2):
                cols = slice(h * 128, (h + 1) * 128)
                st = sbuf[rows, cols]
                is_pos = pos_t[rows, :] == key_id[:, cols]
                one = jnp.where(is_pos, 1.0, 0.0)
                w = jnp.exp2(st * EXP2_SCALE) * jnp.maximum(one, amb[b:b + 1, cols])
                sums.append(w)
                picked.append(st * one)
                to = slice(t * 256 + h * 128, t * 256 + h * 128 + 128)
                wbuf[rows, to] = w.astype(BF16)
                obuf[rows, to] = one.astype(BF16)
            tot[rows, :] += sums[0] + sums[1]
            pss[rows, :] += picked[0] + picked[1]

    def column(first, units, n):
        cols = slice(n * 256, (n + 1) * 256)
        keys = kb[first * 4:(first + units) * 4, :, :, cols].reshape(units * 256, 256)
        e_new = jnp.dot(wbuf[:, 0:units * 256], keys, preferred_element_type=F32)
        p_new = jnp.dot(obuf[:, 0:units * 256], keys, preferred_element_type=F32)
        if first == 0:
            e_acc[:, cols] = e_new
            p_acc[:, cols] = p_new
        else:
            e_acc[:, cols] += e_new
            p_acc[:, cols] += p_new

    def scores(stage):
        ks = STAGES[stage]
        steps = []
        for part in ks:
            for s in (0, 1):
                steps += [functools.partial(score, unit_of(ks[0][0]), len(steps) + i, s, k) for i, k in enumerate(part)]
        return steps

    def columns(stage):
        units = 2 * sum(len(part) for part in STAGES[stage])
        return [functools.partial(column, unit_of(STAGES[stage][0][0]), units, n) for n in range(4)]

    def run(first, second=()):
        first, second = list(first), list(second)
        done = 0
        for i, step in enumerate(first):
            step()
            upto = (i + 1) * len(second) // len(first)
            for other in second[done:upto]:
                other()
            done = upto

    def wholes(r):
        return [functools.partial(whole, k) for k in ((r, 8 - r) if r < 4 else (4,))]

    def halves(r, js=(1, 3, 2)):
        return [functools.partial(half, k, j) for j in js for k in ((r, 8 - r) if r < 4 else (4,))]

    def events(r):
        return wholes(r) + halves(r)

    cluster_rows()
    near(1)
    near(3)
    near(2)
    for d in (1, 3, 2):
        send(("xb", d), kb.at[0, 1], kb.at[d, 1], at_x(d))
    run(wholes(1) + halves(1, (1,)))
    queries_on()
    run(halves(1, (3, 2)))
    share(0)
    prepare()
    run(events(2), scores(0) + columns(0))
    share(1)
    run(events(3), scores(1) + columns(1))
    share(2)
    run(wholes(4) + halves(4, (1,)), scores(2))
    share(3)
    run(columns(2))
    last = scores(3)
    run(halves(4, (3,)), last[:2])
    share(4)
    run(halves(4, (2,)), last[2:4])
    run(last[4:])

    for b in range(4):
        rows = slice(b * 128, (b + 1) * 128)
        tb[0, 0, b:b + 1, :] = jnp.sum(tot[rows, :].T, axis=0, keepdims=True)
    for d in (2, 1, 3):
        send(("tot", d), tb.at[0, 0], tb.at[d, 0], at_y(d))
    for b in range(4):
        rows = slice(b * 128, (b + 1) * 128)
        tb[0, 1, b:b + 1, :] = jnp.sum(pss[rows, :].T, axis=0, keepdims=True)
    for d in (2, 1, 3):
        send(("ps", d), tb.at[0, 1], tb.at[d, 1], at_y(d))

    def total_row(b, base):
        row = tb[0, base, b:b + 1, :]
        for d in (1, 2, 3):
            i = (b - d) % 4
            row = row + tb[d, base, i:i + 1, :]
        return row

    def partial_rows(b, cols):
        rows = slice(b * 128, (b + 1) * 128)
        inverse = jnp.concatenate([tot[rows, :]] * 2, axis=1)
        return e_acc[rows, cols] * inverse - p_acc[rows, cols]

    upper, lower = slice(0, 64), slice(64, 128)

    def leave(n):
        cols = slice(n * 256, (n + 1) * 256)
        pb[2, n] = partial_rows(2, cols).astype(BF16)
        send(("rel", n, 0), pb.at[2, n, upper], rl.at[0, n], at_y(-1))
        send(("rel", n, 1), pb.at[2, n, lower], rl.at[1, n], at_y(1))
        near_y = partial_rows(1, cols)
        pb[0, n, lower] = near_y[lower].astype(BF16)
        send(("out", 1, n, 1), pb.at[0, n, lower], rb.at[0, n, lower], at_y(-1))
        far_y = partial_rows(3, cols)
        pb[1, n, upper] = far_y[upper].astype(BF16)
        send(("out", 3, n, 0), pb.at[1, n, upper], rb.at[1, n, upper], at_y(1))

    def pass_on(n):
        cols = slice(n * 256, (n + 1) * 256)
        arrived("rel", n, 0)
        pb[0, n, upper] = (partial_rows(1, cols)[upper] + rl[0, n].astype(F32)).astype(BF16)
        send(("out", 1, n, 0), pb.at[0, n, upper], rb.at[0, n, upper], at_y(-1))
        arrived("rel", n, 1)
        pb[1, n, lower] = (partial_rows(3, cols)[lower] + rl[1, n].astype(F32)).astype(BF16)
        send(("out", 3, n, 1), pb.at[1, n, lower], rb.at[1, n, lower], at_y(1))

    final = columns(3)
    run(final[:2])
    for d in (1, 3, 2):
        arrived("tot", d)
    for b in (2, 1, 3, 0):
        tot[b * 128:(b + 1) * 128, :] = (1.0 / jnp.broadcast_to(total_row(b, 0), (128, 128))).T
    leave(0)
    leave(1)
    final[2]()
    leave(2)
    final[3]()
    leave(3)
    pass_on(0)
    pass_on(1)
    pass_on(2)
    pass_on(3)
    for d in (1, 3, 2):
        arrived("ps", d)
    ol_ref[...] = jnp.log(total_row(0, 0)) - total_row(0, 1) * 10.0
    scale = (jnp.broadcast_to(lmv[...], (128, 128)).T)[:, 0:1] * 10.0
    projection = jnp.zeros((128, 1), F32)
    for n in range(4):
        cols = slice(n * 256, (n + 1) * 256)
        for b in (1, 3):
            for h in (0, 1):
                arrived("out", b, n, h)
        direction = partial_rows(0, cols) + (rb[0, n].astype(F32) + rb[1, n].astype(F32))
        g = direction * scale
        og_ref[:, cols] = g
        projection = projection + jnp.sum(qin[:, cols].astype(F32) * g, axis=1, keepdims=True)
    xf = qin[...].astype(F32)
    q_scale = lax.rsqrt(jnp.sum(xf * xf, axis=1, keepdims=True) + EPS)
    og_ref[...] = q_scale * og_ref[...] - (q_scale * q_scale * q_scale * projection) * xf
    for copy in copies.values():
        copy.wait_send()


def body(queries, keys, pattern, clusters, positives, loss_multiplier):
    hbm = pl.BlockSpec(memory_space=pltpu.HBM)
    vmem = pl.BlockSpec(memory_space=pltpu.VMEM)
    count = len(IDS.names)
    grad, loss = pl.pallas_call(
        kernel,
        out_shape=(jax.ShapeDtypeStruct((128, 1024), F32), jax.ShapeDtypeStruct((1, 128), F32)),
        in_specs=[hbm] * 6,
        out_specs=(vmem, vmem),
        scratch_shapes=[
            pltpu.VMEM((64, 1024), BF16),
            pltpu.VMEM((128, 1024), BF16),
            pltpu.VMEM((1, 64), I32),
            pltpu.VMEM((1, 128), F32),
            pltpu.VMEM((64, 2, 32, 1024), BF16),
            pltpu.VMEM((4, 128, 1024), BF16),
            pltpu.VMEM((4, 1, 384), I32),
            pltpu.VMEM((4, 1, 256), I32),
            pltpu.VMEM((2, 8, 1, 256), I32),
            pltpu.VMEM((8, 256), F32),
            pltpu.VMEM((8, 256), F32),
            pltpu.VMEM((512, 1536), BF16),
            pltpu.VMEM((512, 1536), BF16),
            pltpu.VMEM((512, 256), F32),
            pltpu.VMEM((512, 1024), F32),
            pltpu.VMEM((512, 1024), F32),
            pltpu.VMEM((512, 128), F32),
            pltpu.VMEM((512, 128), F32),
            pltpu.VMEM((512, 128), F32),
            pltpu.VMEM((4, 2, 8, 128), F32),
            pltpu.VMEM((3, 4, 128, 256), BF16),
            pltpu.VMEM((2, 4, 128, 256), BF16),
            pltpu.VMEM((2, 4, 64, 256), BF16),
            pltpu.SemaphoreType.DMA((6,)),
            pltpu.SemaphoreType.DMA((count,)),
            pltpu.SemaphoreType.DMA((count,)),
        ],
        compiler_params=pltpu.CompilerParams(
            collective_id=0, has_side_effects=True, vmem_limit_bytes=63 * 1024 * 1024 + 768 * 1024),
        name="contrastive",
    )(queries, keys, pattern, clusters.reshape(1, 64), positives.reshape(1, 128), loss_multiplier.reshape(1, 128))
    return grad, loss.reshape(128)


def solution(mesh):
    rows, flat = P(("dp", "index"), None), P(("dp", "index"))
    return jax.shard_map(
        body, mesh=mesh, in_specs=(rows, rows, rows, flat, flat, flat), out_specs=(rows, flat), check_vma=False)
```

```python
import functools
import math

import jax
import jax.numpy as jnp
from jax import lax
from jax.experimental import pallas as pl
from jax.experimental.pallas import tpu as pltpu
from jax.sharding import PartitionSpec as P

MESH = pl.DeviceIdType.MESH
EPS = 1e-06
NX, NY, NZ = 4, 4, 8
EXP2_SCALE = 10.0 * math.log2(math.e)
F32, BF16, I32 = jnp.float32, jnp.bfloat16, jnp.int32


def unit_of(k):
    if k == 0:
        return 0
    if k == 4:
        return 14
    return 2 + 4 * (k - 1) if k < 4 else 2 + 4 * (7 - k) + 1


def sibling_unit(k):
    return unit_of(k) + (1 if k in (0, 4) else 2)


class Ids:
    def __init__(self):
        self.names = {}

    def __call__(self, *name):
        return self.names.setdefault(name, len(self.names))


def message_names():
    ids = Ids()
    for d in (1, 2, 3):
        ids("xa", d), ids("xb", d), ids("cx", d), ids("meta", d), ids("tot", d), ids("ps", d)
    for name in (("q", 1), ("q", 3), ("q2", 1), ("q2", 3), ("cs",)):
        ids(*name)
    for k in range(1, 8):
        ids("cz", k), ids("f", k)
        for d in (1, 2, 3):
            ids("bx", k, d), ids("g", k, d)
    for k in range(8):
        if k != 4:
            ids("sib", k)
    ids("sw"), ids("sg", 0), ids("sg", 1), ids("sg", 2), ids("sg", 3)
    for n in range(4):
        for h in (0, 1):
            ids("rel", n, h), ids("out", 1, n, h), ids("out", 3, n, h)
    return ids


IDS = message_names()
STAGES = (((0,),), ((1, 7),), ((2, 6),), ((3, 5), (4,)))


def kernel(q_ref, k_ref, pat_ref, cl_ref, pos_ref, lm_ref, og_ref, ol_ref, kin, qin, clv, lmv, kb, qb, mb, clx, clz,
           pm, amb, wbuf, obuf, sbuf, e_acc, p_acc, pos_t, tot, pss, tb, pb, rb, rl, lsem, ssem, rsem):
    dp, ix = lax.axis_index("dp"), lax.axis_index("index")
    c, y, x, z = dp % 2, (dp // 2) % NY, (ix % 2) * 2 + dp // (2 * NY), ix // 2

    def dev(xx, yy, zz, cc):
        return ((xx % 2) * NY + yy) * 2 + cc, zz * 2 + xx // 2

    def at_x(d):
        return dev((x + d + NX) % NX, y, z, c)

    def at_y(d):
        return dev(x, (y + d + NY) % NY, z, c)

    def at_z(d):
        return dev(x, y, (z + d + NZ) % NZ, c)

    sibling = dev(x, y, z, 1 - c)
    partners = [at_x(d) for d in (1, 2, 3)] + [at_y(d) for d in (1, 2, 3)] + [at_z(d) for d in range(1, 8)] + [sibling]

    barrier = pltpu.get_barrier_semaphore()
    for partner in partners:
        pl.semaphore_signal(barrier, inc=1, device_id=partner, device_id_type=MESH)

    copies = {}

    def send(name, src, dst, target):
        number = IDS.names[name]
        copy = pltpu.make_async_remote_copy(
            src_ref=src, dst_ref=dst, send_sem=ssem.at[number], recv_sem=rsem.at[number],
            device_id=target, device_id_type=MESH)
        copy.start()
        copies[name] = copy

    def arrived(*name):
        copies[name].wait_recv()

    loads = [
        pltpu.make_async_copy(k_ref, kin, lsem.at[0]),
        pltpu.make_async_copy(q_ref, qin, lsem.at[1]),
        pltpu.make_async_copy(pat_ref, mb.at[0, :, 0:256], lsem.at[2]),
        pltpu.make_async_copy(pos_ref, mb.at[0, :, 256:384], lsem.at[3]),
        pltpu.make_async_copy(cl_ref, clv, lsem.at[4]),
        pltpu.make_async_copy(lm_ref, lmv, lsem.at[5]),
    ]
    for load in loads:
        load.start()
    for load in loads:
        load.wait()
    spread = lax.broadcasted_iota(I32, (64, 256), 0) == lax.broadcasted_iota(I32, (64, 256), 1) % 64
    clx[0] = jnp.dot(jnp.broadcast_to(clv[...].astype(F32), (8, 64)).astype(BF16), spread.astype(F32).astype(BF16),
                     preferred_element_type=F32)[0:1].astype(I32)
    kf = kin[...].astype(F32)
    kn = (kf * lax.rsqrt(jnp.sum(kf * kf, axis=1, keepdims=True) + EPS)).astype(BF16)
    kb[0, 0] = kn[:32]
    kb[0, 1] = kn[32:]
    xf = qin[...].astype(F32)
    qb[0] = (xf * lax.rsqrt(jnp.sum(xf * xf, axis=1, keepdims=True) + EPS)).astype(BF16)
    pl.semaphore_wait(barrier, len(partners))

    def g_half(k, j):
        return kb.at[unit_of(k) * 4 + j, 0]

    def send_g(k, j, source):
        send(("g", k, j), source, g_half(k, j), at_z(1 if k < 4 else -1))

    def send_f(k, source):
        send(("f", k), source, kb.at[unit_of(k) * 4], at_z(1 if k <= 4 else -1))

    def b_half(k, j):
        return kb.at[unit_of(k) * 4 + j, 1]

    for d in (1, 3, 2):
        send(("cx", d), clx.at[0], clx.at[d], at_x(d))
        send(("xa", d), kb.at[0, 0], kb.at[d, 0], at_x(d))
    send_f(1, kb.at[0])
    send_f(7, kb.at[0])
    send(("q", 1), qb.at[0], qb.at[1], at_y(1))
    send(("q", 3), qb.at[0], qb.at[3], at_y(-1))
    for d in (1, 2, 3):
        send(("meta", d), mb.at[0], mb.at[d], at_y(d))

    def near(j):
        arrived("xa", j)
        send_g(1, j, kb.at[j, 0])
        send_g(7, j, kb.at[j, 0])

    def cluster_rows():
        for d in (1, 2, 3):
            arrived("cx", d)
        lane = lax.broadcasted_iota(I32, (1, 256), 1)
        row = clx[0]
        for d in (1, 2, 3):
            row = jnp.where(lane // 64 == d, clx[d], row)
        clz[0, 0] = row
        for k in range(1, 8):
            send(("cz", k), clz.at[0, 0], clz.at[0, k], at_z(k))

    def whole(k):
        arrived("f", k)
        if k < 4:
            send_f(k + 1, kb.at[unit_of(k) * 4])
        elif k > 5:
            send_f(k - 1, kb.at[unit_of(k) * 4])
        for d in (1, 3, 2):
            send(("bx", k, d), b_half(k, 0), b_half(k, d), at_x(d))

    def to_sibling(j):
        u, v = unit_of(4) * 4 + j, sibling_unit(4) * 4 + j
        send(("sg", j), kb.at[u, 0], kb.at[v, 0], sibling)

    def half(k, j):
        arrived("g", k, j)
        if k == 4:
            to_sibling(j)
        if k < 3:
            send_g(k + 1, j, g_half(k, j))
        elif k > 4:
            send_g(k - 1, j, g_half(k, j))

    def share(r):
        for k in (r, 8 - r) if 0 < r < 4 else (r,):
            for d in (1, 3, 2):
                if k:
                    arrived("bx", k, d)
                else:
                    arrived("xb", d)
            if k == 4:
                to_sibling(0)
                u, v = unit_of(4) * 4, sibling_unit(4) * 4
                send(("sw",), kb.at[u:u + 4, 1], kb.at[v:v + 4, 1], sibling)
                continue
            send(("sib", k), kb.at[pl.ds(unit_of(k) * 4, 4)], kb.at[pl.ds(sibling_unit(k) * 4, 4)], sibling)

    def queries_on():
        arrived("q", 1)
        send(("q2", 1), qb.at[1, 0:64], qb.at[2, 0:64], at_y(1))
        arrived("q", 3)
        send(("q2", 3), qb.at[3, 64:128], qb.at[2, 64:128], at_y(-1))

    def prepare():
        for k in range(1, 8):
            arrived("cz", k)
        send(("cs",), clz.at[0], clz.at[1], sibling)
        pm[...] = jnp.zeros_like(pm)
        for d in range(4):
            if d:
                arrived("meta", d)
            pm[d:d + 1, :] = mb[d, :, 0:256].astype(F32)
            pos = jnp.broadcast_to(mb[d, :, 256:384].astype(F32), (128, 128))
            pos_t[d * 128:(d + 1) * 128, :] = pos.T
        tot[...] = jnp.zeros_like(tot)
        pss[...] = jnp.zeros_like(pss)
        arrived("cs")
        arrived("q2", 1)
        arrived("q2", 3)

    def score(first, t, s, k):
        if s == 1 and k == 4:
            arrived("sw")
            for j in range(4):
                arrived("sg", j)
        elif s == 1:
            arrived("sib", k)
        unit = first + t
        keys = kb[unit * 4:unit * 4 + 4].reshape(256, 1024)
        sbuf[...] = lax.dot_general(qb[...].reshape(512, 1024), keys, (((1,), (1,)), ((), ())),
                                    preferred_element_type=F32)
        lanes = lax.broadcasted_iota(I32, (1, 256), 1)
        xx = (x - lanes // 64 + NX) % NX
        zz = (z - k + NZ) % NZ
        cc = c + s - 2 * c * s
        rank = (((xx % 2) * NY + y) * 2 + cc) * 16 + zz * 2 + xx // 2
        key_id = (rank * 64 + lanes % 64).astype(F32)
        hot = (lax.broadcasted_iota(I32, (256, 256), 0) == clz[s, k]).astype(F32).astype(BF16)
        amb[...] = lax.dot_general(pm[...].astype(BF16), hot, (((1,), (0,)), ((), ())),
                                   preferred_element_type=F32)
        for b in range(4):
            rows = slice(b * 128, (b + 1) * 128)
            sums, picked = [], []
            for h in range(2):
                cols = slice(h * 128, (h + 1) * 128)
                st = sbuf[rows, cols]
                is_pos = pos_t[rows, :] == key_id[:, cols]
                one = jnp.where(is_pos, 1.0, 0.0)
                w = jnp.exp2(st * EXP2_SCALE) * jnp.maximum(one, amb[b:b + 1, cols])
                sums.append(w)
                picked.append(st * one)
                to = slice(t * 256 + h * 128, t * 256 + h * 128 + 128)
                wbuf[rows, to] = w.astype(BF16)
                obuf[rows, to] = one.astype(BF16)
            tot[rows, :] += sums[0] + sums[1]
            pss[rows, :] += picked[0] + picked[1]

    def column(first, units, n):
        cols = slice(n * 256, (n + 1) * 256)
        keys = kb[first * 4:(first + units) * 4, :, :, cols].reshape(units * 256, 256)
        e_new = jnp.dot(wbuf[:, 0:units * 256], keys, preferred_element_type=F32)
        p_new = jnp.dot(obuf[:, 0:units * 256], keys, preferred_element_type=F32)
        if first == 0:
            e_acc[:, cols] = e_new
            p_acc[:, cols] = p_new
        else:
            e_acc[:, cols] += e_new
            p_acc[:, cols] += p_new

    def scores(stage):
        ks = STAGES[stage]
        steps = []
        for part in ks:
            for s in (0, 1):
                steps += [functools.partial(score, unit_of(ks[0][0]), len(steps) + i, s, k) for i, k in enumerate(part)]
        return steps

    def columns(stage):
        units = 2 * sum(len(part) for part in STAGES[stage])
        return [functools.partial(column, unit_of(STAGES[stage][0][0]), units, n) for n in range(4)]

    def run(first, second=()):
        first, second = list(first), list(second)
        done = 0
        for i, step in enumerate(first):
            step()
            upto = (i + 1) * len(second) // len(first)
            for other in second[done:upto]:
                other()
            done = upto

    def wholes(r):
        return [functools.partial(whole, k) for k in ((r, 8 - r) if r < 4 else (4,))]

    def halves(r, js=(1, 3, 2)):
        return [functools.partial(half, k, j) for j in js for k in ((r, 8 - r) if r < 4 else (4,))]

    def events(r):
        return wholes(r) + halves(r)

    cluster_rows()
    near(1)
    near(3)
    near(2)
    for d in (1, 3, 2):
        send(("xb", d), kb.at[0, 1], kb.at[d, 1], at_x(d))
    run(wholes(1) + halves(1, (1,)))
    queries_on()
    run(halves(1, (3, 2)))
    share(0)
    prepare()
    run(events(2), scores(0) + columns(0))
    share(1)
    run(events(3), scores(1) + columns(1)[:2])
    share(2)
    run(columns(1)[2:])
    run(wholes(4) + halves(4, (1,)), scores(2))
    share(3)
    run(columns(2))
    last = scores(3)
    run(halves(4, (3,)), last[:2])
    share(4)
    run(halves(4, (2,)), last[2:4])
    run(last[4:])

    for b in range(4):
        rows = slice(b * 128, (b + 1) * 128)
        tb[0, 0, b:b + 1, :] = jnp.sum(tot[rows, :].T, axis=0, keepdims=True)
    for d in (2, 1, 3):
        send(("tot", d), tb.at[0, 0], tb.at[d, 0], at_y(d))
    for b in range(4):
        rows = slice(b * 128, (b + 1) * 128)
        tb[0, 1, b:b + 1, :] = jnp.sum(pss[rows, :].T, axis=0, keepdims=True)
    for d in (2, 1, 3):
        send(("ps", d), tb.at[0, 1], tb.at[d, 1], at_y(d))

    def total_row(b, base):
        row = tb[0, base, b:b + 1, :]
        for d in (1, 2, 3):
            i = (b - d) % 4
            row = row + tb[d, base, i:i + 1, :]
        return row

    def partial_rows(b, cols):
        rows = slice(b * 128, (b + 1) * 128)
        inverse = jnp.concatenate([tot[rows, :]] * 2, axis=1)
        return e_acc[rows, cols] * inverse - p_acc[rows, cols]

    upper, lower = slice(0, 64), slice(64, 128)

    def leave(n):
        cols = slice(n * 256, (n + 1) * 256)
        pb[2, n] = partial_rows(2, cols).astype(BF16)
        send(("rel", n, 0), pb.at[2, n, upper], rl.at[0, n], at_y(-1))
        send(("rel", n, 1), pb.at[2, n, lower], rl.at[1, n], at_y(1))
        near_y = partial_rows(1, cols)
        pb[0, n, lower] = near_y[lower].astype(BF16)
        send(("out", 1, n, 1), pb.at[0, n, lower], rb.at[0, n, lower], at_y(-1))
        far_y = partial_rows(3, cols)
        pb[1, n, upper] = far_y[upper].astype(BF16)
        send(("out", 3, n, 0), pb.at[1, n, upper], rb.at[1, n, upper], at_y(1))

    def pass_on(n):
        cols = slice(n * 256, (n + 1) * 256)
        arrived("rel", n, 0)
        pb[0, n, upper] = (partial_rows(1, cols)[upper] + rl[0, n].astype(F32)).astype(BF16)
        send(("out", 1, n, 0), pb.at[0, n, upper], rb.at[0, n, upper], at_y(-1))
        arrived("rel", n, 1)
        pb[1, n, lower] = (partial_rows(3, cols)[lower] + rl[1, n].astype(F32)).astype(BF16)
        send(("out", 3, n, 1), pb.at[1, n, lower], rb.at[1, n, lower], at_y(1))

    final = columns(3)
    run(final[:3])
    for d in (1, 3, 2):
        arrived("tot", d)
    for b in (2, 1, 3, 0):
        tot[b * 128:(b + 1) * 128, :] = (1.0 / jnp.broadcast_to(total_row(b, 0), (128, 128))).T
    leave(0)
    leave(1)
    leave(2)
    final[3]()
    leave(3)
    for n in range(4):
        og_ref[:, n * 256:(n + 1) * 256] = partial_rows(0, slice(n * 256, (n + 1) * 256))
    own = qin[...].astype(F32)
    q_scale = lax.rsqrt(jnp.sum(own * own, axis=1, keepdims=True) + EPS)
    scale = (jnp.broadcast_to(lmv[...], (128, 128)).T)[:, 0:1] * 10.0
    pass_on(0)
    pass_on(1)
    pass_on(2)
    pass_on(3)
    for d in (1, 3, 2):
        arrived("ps", d)
    ol_ref[...] = jnp.log(total_row(0, 0)) - total_row(0, 1) * 10.0
    projection = jnp.zeros((128, 1), F32)
    for n in range(4):
        cols = slice(n * 256, (n + 1) * 256)
        for b in (1, 3):
            for h in (0, 1):
                arrived("out", b, n, h)
        direction = og_ref[:, cols] + (rb[0, n].astype(F32) + rb[1, n].astype(F32))
        g = direction * scale
        og_ref[:, cols] = g
        projection = projection + jnp.sum(qin[:, cols].astype(F32) * g, axis=1, keepdims=True)
    xf = qin[...].astype(F32)
    og_ref[...] = q_scale * og_ref[...] - (q_scale * q_scale * q_scale * projection) * xf
    for copy in copies.values():
        copy.wait_send()


def body(queries, keys, pattern, clusters, positives, loss_multiplier):
    hbm = pl.BlockSpec(memory_space=pltpu.HBM)
    vmem = pl.BlockSpec(memory_space=pltpu.VMEM)
    count = len(IDS.names)
    grad, loss = pl.pallas_call(
        kernel,
        out_shape=(jax.ShapeDtypeStruct((128, 1024), F32), jax.ShapeDtypeStruct((1, 128), F32)),
        in_specs=[hbm] * 6,
        out_specs=(vmem, vmem),
        scratch_shapes=[
            pltpu.VMEM((64, 1024), BF16),
            pltpu.VMEM((128, 1024), BF16),
            pltpu.VMEM((1, 64), I32),
            pltpu.VMEM((1, 128), F32),
            pltpu.VMEM((64, 2, 32, 1024), BF16),
            pltpu.VMEM((4, 128, 1024), BF16),
            pltpu.VMEM((4, 1, 384), I32),
            pltpu.VMEM((4, 1, 256), I32),
            pltpu.VMEM((2, 8, 1, 256), I32),
            pltpu.VMEM((8, 256), F32),
            pltpu.VMEM((8, 256), F32),
            pltpu.VMEM((512, 1536), BF16),
            pltpu.VMEM((512, 1536), BF16),
            pltpu.VMEM((512, 256), F32),
            pltpu.VMEM((512, 1024), F32),
            pltpu.VMEM((512, 1024), F32),
            pltpu.VMEM((512, 128), F32),
            pltpu.VMEM((512, 128), F32),
            pltpu.VMEM((512, 128), F32),
            pltpu.VMEM((4, 2, 8, 128), F32),
            pltpu.VMEM((3, 4, 128, 256), BF16),
            pltpu.VMEM((2, 4, 128, 256), BF16),
            pltpu.VMEM((2, 4, 64, 256), BF16),
            pltpu.SemaphoreType.DMA((6,)),
            pltpu.SemaphoreType.DMA((count,)),
            pltpu.SemaphoreType.DMA((count,)),
        ],
        compiler_params=pltpu.CompilerParams(
            collective_id=0, has_side_effects=True, vmem_limit_bytes=63 * 1024 * 1024 + 768 * 1024),
        name="contrastive",
    )(queries, keys, pattern, clusters.reshape(1, 64), positives.reshape(1, 128), loss_multiplier.reshape(1, 128))
    return grad, loss.reshape(128)


def solution(mesh):
    rows, flat = P(("dp", "index"), None), P(("dp", "index"))
    return jax.shard_map(
        body, mesh=mesh, in_specs=(rows, rows, rows, flat, flat, flat), out_specs=(rows, flat), check_vma=False)
```
